1024 devices in a mesh: beam: 16 (over z, core), lat: 64 (over x, y).
Axes of the slice: x: 8, y: 8, z: 8, core: 2. Of those that a mesh axis runs over, the one named last changes fastest.
Arguments:
- contrast: float32 [2, 16, 8192, 256], P(None, 'beam', 'lat'), may hold values from -0.15 to 0.15
- probe: float32 [2, 128, 128], replicated, may hold values from -6 to 6
- offset_x: int32 [512], P('lat'), may hold values from 0 to 127
- offset_y: int32 [512], P('lat'), may hold values from 0 to 128
- probe_count: int32 [64], P('lat'), may hold values from 1 to 8, 384 in all
- measured: float32 [512, 128, 128], P('lat'), may hold values from 0 to 4
Outputs:
- object_gradient: float32 [2, 16, 8192, 256], P(None, 'beam', 'lat')
The draws below stay inside these ranges and needn't reach their ends.
Inputs may be any that keep to these rules, and one draw needn't show every extreme that they name: `probe_count`: slots below this count hold probes; the others hold none and add nothing; some lat index has all 8. `offset_x`: a probe's block may reach into the next lat index's columns.
All inputs are finite; a program needn't handle non-finite values. No bound on the sum of `probe_count` on one device may be relied on, other than what follows from the above.
Results may differ from the reference program's by a relative error of at most 0.038.
Values may be sent and summed in bfloat16 or wider, within the bound.
A program may use at most 32 MiB of HBM per device.

```python
import math
import jax
import jax.numpy as jnp
import numpy as np
from jax import lax

PATCH = 128
SLICES = 1
TILE = 128
HEIGHT = 256
SLOTS = 8
NZ = 16
NX = 8192
PROBES = 512
N_BEAM = 16
N_LAT = 64


def with_ends(drawn, key, smallest, largest):
    extent = drawn.shape
    spot = [jax.random.randint(jax.random.fold_in(key, axis), (), 0, extent[axis]) for axis in range(len(extent))]
    drawn = drawn.at[tuple(spot)].set(smallest)
    longest = extent.index(max(extent))
    spot[longest] = (spot[longest] + 1) % extent[longest]
    return drawn.at[tuple(spot)].set(largest)


def block_levels(stream_key, extent, cuts, least, high):
    def one(dim, blocks):
        steps = jax.random.uniform(jax.random.fold_in(jax.random.fold_in(stream_key, 6), dim), (blocks,), jnp.float32, least / len(cuts), high / len(cuts))
        return jnp.repeat(jnp.exp(steps), extent[dim] // blocks).reshape((-1,) + (1,) * (len(extent) - dim - 1))

    gain = one(*cuts[0])
    for cut in cuts[1:]:
        gain = gain * one(*cut)
    return gain


def split_up(number_of, total, limit, lean):
    loads = [(1 << 20) // math.isqrt(standing ** lean) + 1 for standing in range(2, number_of + 1)]
    spare, counts = total - limit - (number_of - 1), [1] * (number_of - 1)
    while spare > 0:
        candidates = [i for i in range(number_of - 1) if counts[i] < limit]
        pool, remaining = sum([loads[i] for i in candidates]), spare
        for i in candidates:
            more = min(limit - counts[i], max(1, remaining * loads[i] // pool), spare)
            counts[i] = counts[i] + more
            spare = spare - more
    return np.array([limit] + counts)


def ragged(rng, amount, total, limit, skew):
    if amount == 2:
        one = jax.random.randint(rng, (), max(1, total - limit), min(limit, total - 1) + 1)
        return jnp.stack([one, total - one])
    tallies = jnp.asarray(split_up(amount, total, limit, skew), jnp.int32)
    couples = (amount - 1) // 2
    giver, taker = tallies[1:1 + 2 * couples:2], tallies[2:2 + 2 * couples:2]
    margin = jnp.minimum(giver - 1, limit - taker)
    moved = jax.random.randint(jax.random.fold_in(rng, 1), (couples,), 0, 1 << 20) % (margin + 1)
    tallies = tallies.at[1:1 + 2 * couples:2].set(giver - moved).at[2:2 + 2 * couples:2].set(taker + moved)
    return tallies[jax.random.permutation(jax.random.fold_in(rng, 2), amount)]


def normal_values(key, dims, scale, reach, held_as=jnp.bfloat16):
    values = scale * jax.random.normal(key, dims, jnp.float32)
    return jnp.clip(values, min=-reach, max=reach).astype(held_as)


def setup_inputs(seed: int = 0) -> dict:
    streams_of = jax.random.split(jax.random.key(seed), 7)
    contrast = jnp.clip(jax.random.uniform(streams_of[0], (2, NZ, NX, HEIGHT), jnp.float32, -0.15, 0.15) * block_levels(streams_of[0], (2, NZ, NX, HEIGHT), ((1, 16), (2, 64)), -0.4, 0.0), -0.15, 0.15)
    probe = normal_values(streams_of[1], (2, PATCH, PATCH), 1.0, 6.0, jnp.float32)
    offset_x = with_ends(jax.random.randint(streams_of[2], (PROBES,), 0, TILE), jax.random.fold_in(streams_of[2], 1), 0, TILE - 1).astype(jnp.int32)
    offset_y = with_ends(jax.random.randint(streams_of[3], (PROBES,), 0, HEIGHT - PATCH + 1), jax.random.fold_in(streams_of[3], 1), 0, HEIGHT - PATCH).astype(jnp.int32)
    probe_count = ragged(streams_of[4], N_LAT, 3 * N_LAT * SLOTS // 4, SLOTS, 1).astype(jnp.int32)
    measured = jnp.clip(4.0 * jax.random.uniform(streams_of[5], (PROBES, PATCH, PATCH), jnp.float32) ** block_levels(streams_of[5], (PROBES, PATCH, PATCH), ((0, 64),), -0.2, 0.2), 0.0, 4.0)
    return {"contrast": contrast, "probe": probe, "offset_x": offset_x, "offset_y": offset_y, "probe_count": probe_count, "measured": measured}


def tables(order):
    index = jnp.arange(order, dtype=jnp.int32)
    product = index[:, None] * index[None, :] % order
    theta = product.astype(jnp.float32) * (2.0 * math.pi / order)
    factor = 1.0 / math.sqrt(order)
    shifted = (index + order // 2) % order - order // 2
    quad = (shifted[:, None] * shifted[:, None] + shifted[None, :] * shifted[None, :]) % (4 * order)
    phase = quad.astype(jnp.float32) * (-math.pi / (2 * order))
    return (jnp.cos(theta) * factor, -jnp.sin(theta) * factor, jnp.cos(phase), jnp.sin(phase))

def left_product(matrix, field):
    return jnp.einsum('mn,...nk->...mk', matrix, field, precision=lax.Precision.HIGHEST)

def right_product(field, matrix):
    return jnp.einsum('...mn,nk->...mk', field, matrix, precision=lax.Precision.HIGHEST)

def both_sides(field_re, field_im, matrix_re, matrix_im):
    half_re = left_product(matrix_re, field_re) - left_product(matrix_im, field_im)
    half_im = left_product(matrix_re, field_im) + left_product(matrix_im, field_re)
    full_re = right_product(half_re, matrix_re) - right_product(half_im, matrix_im)
    full_im = right_product(half_re, matrix_im) + right_product(half_im, matrix_re)
    return (full_re, full_im)

def propagate(field_re, field_im, tabs, sign):
    dft_re, dft_im, kernel_re, kernel_im = tabs
    spec_re, spec_im = both_sides(field_re, field_im, dft_re, dft_im)
    signed_im = sign * kernel_im
    mixed_re = spec_re * kernel_re - spec_im * signed_im
    mixed_im = spec_re * signed_im + spec_im * kernel_re
    return both_sides(mixed_re, mixed_im, dft_re, -dft_im)

def far_field(exit_re, exit_im, observed, live, tabs):
    dft_re, dft_im = (tabs[0], tabs[1])
    far_re, far_im = both_sides(exit_re, exit_im, dft_re, dft_im)
    misfit = live[:, None, None] * (far_re * far_re + far_im * far_im - observed)
    return both_sides(misfit * far_re, misfit * far_im, dft_re, -dft_im)

def passed(field):
    return lax.optimization_barrier(field.astype(jnp.bfloat16)).astype(jnp.float32)

def reference(contrast, probe, offset_x, offset_y, probe_count, measured):
    tabs = tables(PATCH)
    padded = jnp.pad(contrast, ((0, 0), (0, 0), (0, PATCH), (0, 0)))
    anchor = jnp.zeros((), jnp.int32)
    groups = jnp.arange(N_BEAM, dtype=jnp.int32)

    def visit(accumulated, lat_item):
        lat_index, corner_x, corner_y, observed = lat_item
        corner_x = corner_x + lat_index * TILE

        def cut_block(x_start, y_start):
            return lax.dynamic_slice(padded, (anchor, anchor, x_start, y_start), (2, NZ, PATCH, PATCH))
        patches = jax.vmap(cut_block)(corner_x, corner_y)
        trans_re = (1.0 + jnp.transpose(patches[:, 0], (1, 0, 2, 3))).reshape(N_BEAM, SLICES, SLOTS, PATCH, PATCH)
        trans_im = jnp.transpose(patches[:, 1], (1, 0, 2, 3)).reshape(N_BEAM, SLICES, SLOTS, PATCH, PATCH)
        live = (jnp.arange(SLOTS, dtype=jnp.int32) < probe_count[lat_index]).astype(jnp.float32)
        start_re = jnp.broadcast_to(probe[0], (SLOTS, PATCH, PATCH))
        start_im = jnp.broadcast_to(probe[1], (SLOTS, PATCH, PATCH))

        def group_forward(wave, group_item):
            group_index, group_re, group_im = group_item
            wave_re, wave_im = wave
            kept_re = []
            kept_im = []
            for layer_index in range(SLICES):
                kept_re.append(wave_re)
                kept_im.append(wave_im)
                mult_re = group_re[layer_index] * wave_re - group_im[layer_index] * wave_im
                mult_im = group_re[layer_index] * wave_im + group_im[layer_index] * wave_re
                wave_re, wave_im = propagate(mult_re, mult_im, tabs, 1.0)
            final = group_index == N_BEAM - 1
            wave_re = jnp.where(final, wave_re, passed(wave_re))
            wave_im = jnp.where(final, wave_im, passed(wave_im))
            return ((wave_re, wave_im), (jnp.stack(kept_re), jnp.stack(kept_im)))
        exits, kept = lax.scan(group_forward, (start_re, start_im), (groups, trans_re, trans_im))
        adjoint = far_field(exits[0], exits[1], observed, live, tabs)

        def group_back(adjoint_now, group_item):
            group_index, group_re, group_im, saved_re, saved_im = group_item
            adj_re, adj_im = adjoint_now
            grads_re = [None] * SLICES
            grads_im = [None] * SLICES
            for layer_index in reversed(range(SLICES)):
                back_re, back_im = propagate(adj_re, adj_im, tabs, -1.0)
                psi_re = saved_re[layer_index]
                psi_im = saved_im[layer_index]
                grads_re[layer_index] = psi_re * back_re + psi_im * back_im
                grads_im[layer_index] = psi_re * back_im - psi_im * back_re
                adj_re, adj_im = (group_re[layer_index] * back_re + group_im[layer_index] * back_im, group_re[layer_index] * back_im - group_im[layer_index] * back_re)
            first_group = group_index == 0
            adj_re = jnp.where(first_group, adj_re, passed(adj_re))
            adj_im = jnp.where(first_group, adj_im, passed(adj_im))
            return ((adj_re, adj_im), (jnp.stack(grads_re), jnp.stack(grads_im)))
        unused, grads = lax.scan(group_back, adjoint, (groups, trans_re, trans_im, kept[0], kept[1]), reverse=True)
        grad_re = grads[0].reshape(NZ, SLOTS, PATCH, PATCH)
        grad_im = grads[1].reshape(NZ, SLOTS, PATCH, PATCH)
        for slot_index in range(SLOTS):
            piece = jnp.stack([grad_re[:, slot_index], grad_im[:, slot_index]])
            place = (anchor, anchor, corner_x[slot_index], corner_y[slot_index])
            current = lax.dynamic_slice(accumulated, place, piece.shape)
            accumulated = lax.dynamic_update_slice(accumulated, current + piece, place)
        return (accumulated, None)
    lat_items = (jnp.arange(N_LAT, dtype=jnp.int32), offset_x.reshape(N_LAT, SLOTS), offset_y.reshape(N_LAT, SLOTS), measured.reshape(N_LAT, SLOTS, PATCH, PATCH))
    accumulated, unused = lax.scan(visit, jnp.zeros(padded.shape, jnp.float32), lat_items)
    return accumulated[:, :, :NX]
```

```python
import functools
import math

import jax
import jax.numpy as jnp
import numpy as np
from jax import lax
from jax.experimental import pallas as pl
from jax.experimental.pallas import tpu as pltpu
from jax.sharding import PartitionSpec as P

MESH = pl.DeviceIdType.MESH
BF16 = jnp.bfloat16
F32 = jnp.float32


def host_tables(order):
    index = np.arange(order)
    dft = np.exp(-2j * np.pi * (np.outer(index, index) % order) / order) / math.sqrt(order)
    shifted = (index + order // 2) % order - order // 2
    phase = np.exp(-1j * np.pi * (shifted * shifted) / (2 * order))
    step = dft.conj() @ (phase[:, None] * dft)

    def halves(matrix):
        right = np.block([[matrix.real, matrix.imag], [-matrix.imag, matrix.real]])
        left = np.block([[matrix.real, -matrix.imag], [matrix.imag, matrix.real]])
        parts = []
        for form in (right, left):
            high = form.astype(np.float32).astype(jnp.bfloat16)
            low = (form - high.astype(np.float64)).astype(np.float32).astype(jnp.bfloat16)
            parts += [high, low]
        return np.stack(parts)

    return halves(step), halves(dft)


def dot(a, b):
    return jnp.dot(a, b, preferred_element_type=F32)


def split(value):
    high = value.astype(BF16)
    return high, (value - high.astype(F32)).astype(BF16)


def sandwich(re, im, tab):
    n = re.shape[0]
    high, low = split(jnp.concatenate([re, im], axis=1))
    half = dot(high, tab[0]) + dot(low, tab[0]) + dot(high, tab[1])
    high, low = split(jnp.concatenate([half[:, :n], half[:, n:]], axis=0))
    full = dot(tab[2], high) + dot(tab[2], low) + dot(tab[3], high)
    return full[:n], full[n:]


def picks(shape, start, along):
    a = lax.broadcasted_iota(jnp.int32, shape, along)
    b = lax.broadcasted_iota(jnp.int32, shape, 1 - along)
    return jnp.where(a == b + start, 1.0, 0.0).astype(BF16)


def kernel(
    ox_ref,
    oy_ref,
    count_ref,
    contrast_ref,
    probe_ref,
    measured_ref,
    step_ref,
    dft_ref,
    out_ref,
    ext,
    blocks,
    trans,
    waves,
    sent,
    landed,
    spread,
    rim_out,
    rim_in,
    block_send,
    block_recv,
    grad_send,
    grad_recv,
    rim_send,
    rim_recv,
    *,
    n_beam,
    n_lat,
):
    slots, n = measured_ref.shape[0], measured_ref.shape[1]
    wide = contrast_ref.shape[3]
    stride = n_beam // slots
    me = lax.axis_index("beam")
    lat = lax.axis_index("lat")
    before = lax.rem(lat + n_lat - 1, n_lat)
    after = lax.rem(lat + 1, n_lat)
    works = lax.rem(me, stride) == 0
    slot = me // stride

    barrier = pltpu.get_barrier_semaphore()
    for other in (before, after):
        pl.semaphore_signal(barrier, inc=1, device_id={"lat": other}, device_id_type=MESH)

    @pl.loop(1, n_beam)
    def _(d):
        other = lax.rem(me + d, n_beam)
        pl.semaphore_signal(barrier, inc=1, device_id={"beam": other}, device_id_type=MESH)

    ext[0:n, 0:wide] = contrast_ref[0, 0].astype(BF16)
    ext[0:n, wide : 2 * wide] = contrast_ref[1, 0].astype(BF16)
    pl.semaphore_wait(barrier, n_beam + 1)

    rim = pltpu.make_async_remote_copy(
        src_ref=ext.at[0:n],
        dst_ref=ext.at[n : 2 * n],
        send_sem=rim_send.at[0],
        recv_sem=rim_recv.at[0],
        device_id={"lat": before},
        device_id_type=MESH,
    )
    rim.start()
    rim.wait_recv()

    def block_copy(j):
        return pltpu.make_async_remote_copy(
            src_ref=blocks.at[j],
            dst_ref=trans.at[me],
            send_sem=block_send.at[j],
            recv_sem=block_recv.at[me],
            device_id={"beam": j * stride},
            device_id_type=MESH,
        )

    @pl.loop(0, slots)
    def _(j):
        rows = picks((n, 2 * n), ox_ref[j], 1)
        columns = picks((wide, n), oy_ref[j], 0)
        beyond = lax.broadcasted_iota(jnp.int32, (n, 2 * wide), 0) + ox_ref[j] >= n
        picked = dot(rows, ext[...])
        picked = jnp.where(beyond & (lat == n_lat - 1), 0.0, picked).astype(BF16)
        blocks[j, 0] = dot(picked[:, 0:wide], columns).astype(BF16)
        blocks[j, 1] = dot(picked[:, wide : 2 * wide], columns).astype(BF16)

        @pl.when(j * stride != me)
        def _():
            block_copy(j).start()

        @pl.when(j * stride == me)
        def _():
            pltpu.make_async_copy(blocks.at[j], trans.at[me], block_recv.at[me]).start()

    def grad_copy(k):
        return pltpu.make_async_remote_copy(
            src_ref=sent.at[k],
            dst_ref=landed.at[slot],
            send_sem=grad_send.at[k],
            recv_sem=grad_recv.at[slot],
            device_id={"beam": k},
            device_id_type=MESH,
        )

    def times_trans(k, re, im):
        t_re = 1.0 + trans[k, 0].astype(F32)
        t_im = trans[k, 1].astype(F32)
        return t_re * re - t_im * im, t_re * im + t_im * re

    def wait_block(k):
        pltpu.make_async_copy(blocks.at[0], trans.at[k], block_recv.at[k]).wait()

    def give(k, d_re, d_im):
        w_re, w_im = waves[k, 0], waves[k, 1]
        sent[k, 0] = (w_re * d_re - w_im * d_im).astype(BF16)
        sent[k, 1] = -(w_re * d_im + w_im * d_re).astype(BF16)

        @pl.when(k != me)
        def _():
            grad_copy(k).start()

        @pl.when(k == me)
        def _():
            pltpu.make_async_copy(sent.at[k], landed.at[slot], grad_recv.at[slot]).start()

    @pl.when(works)
    def _():
        waves[0] = probe_ref[...]

        @pl.loop(0, n_beam - 1)
        def _(k):
            wait_block(k)
            re, im = times_trans(k, waves[k, 0], waves[k, 1])
            re, im = sandwich(re, im, step_ref)
            waves[k + 1, 0] = re
            waves[k + 1, 1] = im

        last = n_beam - 1
        wait_block(last)
        re, im = times_trans(last, waves[last, 0], waves[last, 1])
        re, im = sandwich(re, im, dft_ref)
        live = jnp.where(slot < count_ref[0], 1.0, 0.0)
        misfit = live * (re * re + im * im - measured_ref[slot])
        d_re, d_im = sandwich(misfit * re, -(misfit * im), dft_ref)
        give(last, d_re, d_im)
        re, im = times_trans(last, d_re, d_im)
        waves[last, 0] = re
        waves[last, 1] = im

        @pl.loop(0, last)
        def _(i):
            k = last - 1 - i
            d_re, d_im = sandwich(waves[last, 0], waves[last, 1], step_ref)
            give(k, d_re, d_im)
            re, im = times_trans(k, d_re, d_im)
            waves[last, 0] = re
            waves[last, 1] = im

    @pl.loop(0, slots)
    def _(j):
        pltpu.make_async_copy(sent.at[0], landed.at[j], grad_recv.at[j]).wait()
        columns = picks((n, wide), oy_ref[j], 1)
        spread[j, :, 0:wide] = dot(landed[j, 0], columns).astype(BF16)
        spread[j, :, wide : 2 * wide] = dot(landed[j, 1], columns).astype(BF16)

    def gathered(shift):
        def add(j, total):
            rows = picks((n, n), ox_ref[j] - shift, 0)
            return total + dot(rows, spread[j])

        return lax.fori_loop(0, slots, add, jnp.zeros((n, 2 * wide), F32))

    rim_out[...] = gathered(n).astype(BF16)
    back = pltpu.make_async_remote_copy(
        src_ref=rim_out,
        dst_ref=rim_in,
        send_sem=rim_send.at[1],
        recv_sem=rim_recv.at[1],
        device_id={"lat": after},
        device_id_type=MESH,
    )
    back.start()
    own = gathered(0)
    back.wait_recv()
    own = own + jnp.where(lat == 0, 0.0, rim_in[...].astype(F32))
    out_ref[0, 0] = own[:, 0:wide]
    out_ref[1, 0] = own[:, wide : 2 * wide]

    rim.wait_send()
    back.wait_send()

    @pl.loop(0, slots)
    def _(j):
        @pl.when(j * stride != me)
        def _():
            block_copy(j).wait_send()

    @pl.when(works)
    def _():
        @pl.loop(0, n_beam)
        def _(k):
            @pl.when(k != me)
            def _():
                grad_copy(k).wait_send()


def on_device(n_beam, n_lat, contrast, probe, offset_x, offset_y, probe_count, measured):
    slots, n = measured.shape[0], measured.shape[1]
    wide = contrast.shape[3]
    step, dft = host_tables(n)
    vmem = pl.BlockSpec(memory_space=pltpu.VMEM)
    smem = pl.BlockSpec(memory_space=pltpu.SMEM)
    return pl.pallas_call(
        functools.partial(kernel, n_beam=n_beam, n_lat=n_lat),
        out_shape=jax.ShapeDtypeStruct(contrast.shape, F32),
        in_specs=[smem] * 3 + [vmem] * 5,
        out_specs=vmem,
        scratch_shapes=[
            pltpu.VMEM((2 * n, 2 * wide), BF16),
            pltpu.VMEM((slots, 2, n, n), BF16),
            pltpu.VMEM((n_beam, 2, n, n), BF16),
            pltpu.VMEM((n_beam, 2, n, n), F32),
            pltpu.VMEM((n_beam, 2, n, n), BF16),
            pltpu.VMEM((slots, 2, n, n), BF16),
            pltpu.VMEM((slots, n, 2 * wide), BF16),
            pltpu.VMEM((n, 2 * wide), BF16),
            pltpu.VMEM((n, 2 * wide), BF16),
            pltpu.SemaphoreType.DMA((slots,)),
            pltpu.SemaphoreType.DMA((n_beam,)),
            pltpu.SemaphoreType.DMA((n_beam,)),
            pltpu.SemaphoreType.DMA((slots,)),
            pltpu.SemaphoreType.DMA((2,)),
            pltpu.SemaphoreType.DMA((2,)),
        ],
        compiler_params=pltpu.CompilerParams(
            collective_id=0, has_side_effects=True, vmem_limit_bytes=40 << 20
        ),
    )(offset_x, offset_y, probe_count, contrast, probe, measured, jnp.asarray(step), jnp.asarray(dft))


def solution(mesh):
    in_specs = (
        P(None, "beam", "lat", None),
        P(),
        P("lat"),
        P("lat"),
        P("lat"),
        P("lat", None, None),
    )
    return jax.shard_map(
        functools.partial(on_device, mesh.shape["beam"], mesh.shape["lat"]),
        mesh=mesh,
        in_specs=in_specs,
        out_specs=P(None, "beam", "lat", None),
        check_vma=False,
    )
```

```python
import functools
import math

import jax
import jax.numpy as jnp
import numpy as np
from jax import lax
from jax.experimental import pallas as pl
from jax.experimental.pallas import tpu as pltpu
from jax.sharding import PartitionSpec as P

MESH = pl.DeviceIdType.MESH
BF16 = jnp.bfloat16
F32 = jnp.float32
ROW_BLOCKS = 2


def host_tables(order):
    index = np.arange(order)
    dft = np.exp(-2j * np.pi * (np.outer(index, index) % order) / order) / math.sqrt(order)
    shifted = (index + order // 2) % order - order // 2
    phase = np.exp(-1j * np.pi * (shifted * shifted) / (2 * order))
    step = dft.conj() @ (phase[:, None] * dft)

    def halves(form):
        high = form.astype(np.float32).astype(jnp.bfloat16)
        low = (form - high.astype(np.float64)).astype(np.float32).astype(jnp.bfloat16)
        return np.stack([high, low])

    rights, lefts = [], []
    for matrix in (step, dft):
        re, im = matrix.real, matrix.imag
        rights.append(halves(np.block([[re, im], [-im, re]])))
        rows = np.block([[re, -im], [im, re]]).reshape(2, ROW_BLOCKS, order // ROW_BLOCKS, 2 * order)
        lefts.append(halves(rows.transpose(1, 0, 2, 3).reshape(2 * order, 2 * order)))
    return np.stack(rights), np.stack(lefts)


def dot(a, b):
    return jnp.dot(a, b, preferred_element_type=F32)


def by_right(blocks, right):
    re, im = [], []
    for block_re, block_im in blocks:
        n = block_re.shape[1]
        both = jnp.concatenate([block_re, block_im], axis=1).astype(BF16)
        half = dot(both, right[0]) + dot(both, right[1])
        re.append(half[:, :n].astype(BF16))
        im.append(half[:, n:].astype(BF16))
    return jnp.concatenate(re + im, axis=0)


def by_left(left, half):
    blocks = []
    n = left.shape[1] // (2 * ROW_BLOCKS)
    for b in range(ROW_BLOCKS):
        rows = slice(2 * b * n, 2 * (b + 1) * n)
        both = dot(left[0, rows], half) + dot(left[1, rows], half)
        blocks.append((both[:n], both[n:]))
    return blocks


def picks(shape, start, along):
    a = lax.broadcasted_iota(jnp.int32, shape, along)
    b = lax.broadcasted_iota(jnp.int32, shape, 1 - along)
    return jnp.where(a == b + start, 1.0, 0.0).astype(BF16)


def kernel(
    ox_ref,
    oy_ref,
    count_ref,
    contrast_hbm,
    probe_hbm,
    measured_hbm,
    rights_hbm,
    lefts_hbm,
    out_hbm,
    contrast,
    measured,
    rights,
    lefts,
    ext,
    cut_rows,
    cut_columns,
    put_columns,
    put_rows,
    blocks,
    trans,
    waves,
    half,
    sent,
    landed,
    spread,
    rim_out,
    rim_in,
    out,
    load,
    store,
    block_send,
    block_recv,
    grad_send,
    grad_recv,
    rim_send,
    rim_recv,
    back_send,
    back_recv,
    here,
    *,
    n_beam,
    n_lat,
):
    slots, n = measured_hbm.shape[0], measured_hbm.shape[1]
    wide = contrast_hbm.shape[3]
    stride = n_beam // slots
    me = lax.axis_index("beam")
    lat = lax.axis_index("lat")
    before, after = lat - 1, lat + 1
    has_before, has_after = lat > 0, lat < n_lat - 1

    def hosts(i):
        return lax.rem(i, stride) == 0

    def slot_of(i):
        return i // stride

    def host(j):
        return j * stride

    lower = jnp.where(hosts(me), me, (me + stride - 1) // stride)
    works = hosts(me)
    slot = slot_of(me)

    def meets(i, j):
        return hosts(i) | hosts(j)

    object_load = pltpu.make_async_copy(contrast_hbm, contrast, load.at[0])
    object_load.start()
    loads = [
        pltpu.make_async_copy(probe_hbm, waves.at[0], load.at[1]),
        pltpu.make_async_copy(rights_hbm, rights, load.at[2]),
        pltpu.make_async_copy(lefts_hbm, lefts, load.at[3]),
        pltpu.make_async_copy(measured_hbm.at[slot], measured, load.at[4]),
    ]

    barrier = pltpu.get_barrier_semaphore()
    for there, other in ((has_before, before), (has_after, after)):

        @pl.when(there)
        def _(other=other):
            pl.semaphore_signal(barrier, inc=1, device_id={"lat": other}, device_id_type=MESH)

    @pl.loop(me + 1, n_beam)
    def _(other):
        @pl.when(meets(me, other))
        def _():
            pl.semaphore_signal(barrier, inc=1, device_id={"beam": other}, device_id_type=MESH)

    object_load.wait()
    for part in (0, 1):
        ext[part, 0:n] = contrast[part, 0].astype(BF16)
    pl.semaphore_wait(barrier, lower + jnp.where(has_before & has_after, 2, 1))

    rims = [
        pltpu.make_async_remote_copy(
            src_ref=ext.at[part, 0:n],
            dst_ref=ext.at[part, n : 2 * n],
            send_sem=rim_send.at[part],
            recv_sem=rim_recv.at[part],
            device_id={"lat": before},
            device_id_type=MESH,
        )
        for part in (0, 1)
    ]

    @pl.when(has_before)
    def _():
        for rim in rims:
            rim.start()

    @pl.loop(0, me)
    def _(other):
        @pl.when(meets(me, other))
        def _():
            pl.semaphore_signal(here.at[me], inc=1, device_id={"beam": other}, device_id_type=MESH)

    @pl.when(works)
    def _():
        for copy in loads:
            copy.start()

    @pl.loop(0, slots)
    def _(j):
        x, y = ox_ref[j], oy_ref[j]
        cut_rows[j] = picks((n, 2 * n), x, 1)
        cut_columns[j] = picks((wide, n), y, 0)
        put_columns[j] = picks((n, wide), y, 1)
        put_rows[j, 0] = picks((n, n), x, 0)
        put_rows[j, 1] = picks((n, n), x - n, 0)

    def block_copy(j):
        return pltpu.make_async_remote_copy(
            src_ref=blocks.at[j],
            dst_ref=trans.at[me],
            send_sem=block_send.at[j],
            recv_sem=block_recv.at[me],
            device_id={"beam": host(j)},
            device_id_type=MESH,
        )

    group = 4
    for part in (0, 1):

        @pl.when(has_after)
        def _(part=part):
            rims[part].wait_recv()

        @pl.when(jnp.logical_not(has_after))
        def _(part=part):
            ext[part, n : 2 * n] = jnp.zeros((n, wide), BF16)

        @pl.loop(0, slots // group)
        def _(g, part=part):
            members = [g * group + m for m in range(group)]
            picked = [dot(cut_rows[j], ext[part]).astype(BF16) for j in members]
            picked = [dot(p, cut_columns[j]).astype(BF16) for p, j in zip(picked, members)]
            for p, j in zip(picked, members):
                blocks[j, part] = p
            if part == 1:
                for j in members:

                    @pl.when(host(j) < me)
                    def _(j=j):
                        block_copy(j).start()

                    @pl.when(host(j) == me)
                    def _(j=j):
                        pltpu.make_async_copy(blocks.at[j], trans.at[me], block_recv.at[me]).start()

    @pl.loop(me + 1, n_beam)
    def _(other):
        @pl.when(meets(me, other))
        def _():
            pl.semaphore_wait(here.at[other], 1)

            @pl.when(hosts(other))
            def _():
                block_copy(slot_of(other)).start()

    def grad_copy(k):
        return pltpu.make_async_remote_copy(
            src_ref=sent.at[k],
            dst_ref=landed.at[slot],
            send_sem=grad_send.at[k],
            recv_sem=grad_recv.at[slot],
            device_id={"beam": k},
            device_id_type=MESH,
        )

    tall = n // ROW_BLOCKS

    def times_trans(k, field):
        out = []
        for b, (re, im) in enumerate(field):
            rows = slice(b * tall, (b + 1) * tall)
            t_re = 1.0 + trans[k, 0, rows].astype(F32)
            t_im = trans[k, 1, rows].astype(F32)
            out.append((t_re * re - t_im * im, t_re * im + t_im * re))
        return out

    def wait_block(k):
        pltpu.make_async_copy(blocks.at[0], trans.at[k], block_recv.at[k]).wait()

    def keep(k, field):
        for b, (re, im) in enumerate(field):
            rows = slice(b * tall, (b + 1) * tall)
            waves[k, 0, rows] = re
            waves[k, 1, rows] = im

    def kept(k):
        return [
            (waves[k, 0, b * tall : (b + 1) * tall], waves[k, 1, b * tall : (b + 1) * tall])
            for b in range(ROW_BLOCKS)
        ]

    def give(k, field):
        for b, ((w_re, w_im), (d_re, d_im)) in enumerate(zip(kept(k), field)):
            rows = slice(b * tall, (b + 1) * tall)
            sent[k, 0, rows] = (w_re * d_re - w_im * d_im).astype(BF16)
            sent[k, 1, rows] = -(w_re * d_im + w_im * d_re).astype(BF16)

    def post(k):
        @pl.when(k != me)
        def _():
            grad_copy(k).start()

        @pl.when(k == me)
        def _():
            pltpu.make_async_copy(sent.at[k], landed.at[slot], grad_recv.at[slot]).start()

    @pl.when(works)
    def _():
        for copy in loads:
            copy.wait()
        wait_block(0)
        half[...] = by_right(times_trans(0, kept(0)), rights.at[0])

        @pl.loop(1, n_beam)
        def _(k):
            wait_block(k)
            field = by_left(lefts.at[0], half[...])
            keep(k, field)
            table = k // (n_beam - 1)
            half[...] = by_right(times_trans(k, field), rights.at[table])

        last = n_beam - 1
        live = jnp.where(slot < count_ref[0], 1.0, 0.0)
        field = []
        for b, (re, im) in enumerate(by_left(lefts.at[1], half[...])):
            misfit = live * (re * re + im * im - measured[b * tall : (b + 1) * tall])
            field.append((misfit * re, -(misfit * im)))
        half[...] = by_right(field, rights.at[1])

        @pl.loop(0, last)
        def _(i):
            k = last - i
            field = by_left(lefts.at[(k + 1) // n_beam], half[...])
            half[...] = by_right(times_trans(k, field), rights.at[0])
            give(k, field)
            post(k)

        give(0, by_left(lefts.at[0], half[...]))
        post(0)

    @pl.loop(0, slots)
    def _(j):
        pltpu.make_async_copy(sent.at[0], landed.at[j], grad_recv.at[j]).wait()
        both = jnp.concatenate([landed[j, 0], landed[j, 1]], axis=0)
        both = dot(both, put_columns[j]).astype(BF16)
        place = pl.ds(pl.multiple_of(j * n, n), n)
        spread[0, place] = both[0:n]
        spread[1, place] = both[n : 2 * n]

    def gathered(part, beyond):
        rows = jnp.concatenate([put_rows[j, beyond] for j in range(slots)], axis=1)
        return dot(rows, spread[part])

    backs = [
        pltpu.make_async_remote_copy(
            src_ref=rim_out.at[part],
            dst_ref=rim_in.at[part],
            send_sem=back_send.at[part],
            recv_sem=back_recv.at[part],
            device_id={"lat": after},
            device_id_type=MESH,
        )
        for part in (0, 1)
    ]
    for part in (0, 1):
        rim_out[part] = gathered(part, 1).astype(BF16)

        @pl.when(has_after)
        def _(part=part):
            backs[part].start()

    for part in (0, 1):
        out[part, 0] = gathered(part, 0)

    for part in (0, 1):

        @pl.when(has_before)
        def _(part=part):
            backs[part].wait_recv()
            out[part, 0] += rim_in[part].astype(F32)

        pltpu.make_async_copy(out.at[part], out_hbm.at[part], store.at[part]).start()

    for part in (0, 1):
        pltpu.make_async_copy(out.at[part], out_hbm.at[part], store.at[part]).wait()

        @pl.when(has_before)
        def _(part=part):
            rims[part].wait_send()

        @pl.when(has_after)
        def _(part=part):
            backs[part].wait_send()

    @pl.loop(0, slots)
    def _(j):
        @pl.when(host(j) != me)
        def _():
            block_copy(j).wait_send()

    @pl.when(works)
    def _():
        @pl.loop(0, n_beam)
        def _(k):
            @pl.when(k != me)
            def _():
                grad_copy(k).wait_send()


def on_device(n_beam, n_lat, contrast, probe, offset_x, offset_y, probe_count, measured):
    slots, n = measured.shape[0], measured.shape[1]
    wide = contrast.shape[3]
    rights, lefts = host_tables(n)
    smem = pl.BlockSpec(memory_space=pltpu.SMEM)
    hbm = pl.BlockSpec(memory_space=pltpu.HBM)
    dma = pltpu.SemaphoreType.DMA
    return pl.pallas_call(
        functools.partial(kernel, n_beam=n_beam, n_lat=n_lat),
        out_shape=jax.ShapeDtypeStruct(contrast.shape, F32),
        in_specs=[smem] * 3 + [hbm] * 5,
        out_specs=hbm,
        scratch_shapes=[
            pltpu.VMEM(contrast.shape, F32),
            pltpu.VMEM((n, n), F32),
            pltpu.VMEM(rights.shape, BF16),
            pltpu.VMEM(lefts.shape, BF16),
            pltpu.VMEM((2, 2 * n, wide), BF16),
            pltpu.VMEM((slots, n, 2 * n), BF16),
            pltpu.VMEM((slots, wide, n), BF16),
            pltpu.VMEM((slots, n, wide), BF16),
            pltpu.VMEM((slots, 2, n, n), BF16),
            pltpu.VMEM((slots, 2, n, n), BF16),
            pltpu.VMEM((n_beam, 2, n, n), BF16),
            pltpu.VMEM((n_beam, 2, n, n), F32),
            pltpu.VMEM((2 * n, n), BF16),
            pltpu.VMEM((n_beam, 2, n, n), BF16),
            pltpu.VMEM((slots, 2, n, n), BF16),
            pltpu.VMEM((2, slots * n, wide), BF16),
            pltpu.VMEM((2, n, wide), BF16),
            pltpu.VMEM((2, n, wide), BF16),
            pltpu.VMEM(contrast.shape, F32),
            dma((5,)),
            dma((2,)),
            dma((slots,)),
            dma((n_beam,)),
            dma((n_beam,)),
            dma((slots,)),
            dma((2,)),
            dma((2,)),
            dma((2,)),
            dma((2,)),
            pltpu.SemaphoreType.REGULAR((n_beam,)),
        ],
        compiler_params=pltpu.CompilerParams(
            collective_id=0, has_side_effects=True, vmem_limit_bytes=60 << 20
        ),
    )(offset_x, offset_y, probe_count, contrast, probe, measured, jnp.asarray(rights), jnp.asarray(lefts))


def solution(mesh):
    in_specs = (
        P(None, "beam", "lat", None),
        P(),
        P("lat"),
        P("lat"),
        P("lat"),
        P("lat", None, None),
    )
    return jax.shard_map(
        functools.partial(on_device, mesh.shape["beam"], mesh.shape["lat"]),
        mesh=mesh,
        in_specs=in_specs,
        out_specs=P(None, "beam", "lat", None),
        check_vma=False,
    )
```

```python
import functools
import math

import jax
import jax.numpy as jnp
import numpy as np
from jax import lax
from jax.experimental import pallas as pl
from jax.experimental.pallas import tpu as pltpu
from jax.sharding import PartitionSpec as P

MESH = pl.DeviceIdType.MESH
BF16 = jnp.bfloat16
F32 = jnp.float32
ROW_BLOCKS = 2


def host_tables(order):
    index = np.arange(order)
    dft = np.exp(-2j * np.pi * (np.outer(index, index) % order) / order) / math.sqrt(order)
    shifted = (index + order // 2) % order - order // 2
    phase = np.exp(-1j * np.pi * (shifted * shifted) / (2 * order))
    step = dft.conj() @ (phase[:, None] * dft)

    def halves(form):
        high = form.astype(np.float32).astype(jnp.bfloat16)
        low = (form - high.astype(np.float64)).astype(np.float32).astype(jnp.bfloat16)
        return np.stack([high, low])

    rights, lefts = [], []
    for matrix in (step, dft):
        re, im = matrix.real, matrix.imag
        rights.append(halves(np.block([[re, im], [-im, re]])))
        rows = halves(np.block([re, im])).reshape(2, ROW_BLOCKS, order // ROW_BLOCKS, 2 * order)
        lefts.append(rows.transpose(1, 0, 2, 3).reshape(2 * order, 2 * order))
    return np.stack(rights), np.stack(lefts)


def dot(a, b):
    return jnp.dot(a, b, preferred_element_type=F32)


def by_right(blocks, right):
    halves = []
    for re, im in blocks:
        both = jnp.concatenate([re, im], axis=1).astype(BF16)
        halves.append(dot(both, right[0]) + dot(both, right[1]))
    half = jnp.concatenate(halves, axis=0)
    n = half.shape[0]
    turned = jnp.concatenate([-half[:, n:], half[:, :n]], axis=1)
    return jnp.concatenate([half.astype(BF16), turned.astype(BF16)], axis=0)


def by_left(left, half):
    blocks = []
    n = left.shape[1] // 2
    tall = n // ROW_BLOCKS
    for b in range(ROW_BLOCKS):
        both = dot(left[2 * b * tall : 2 * (b + 1) * tall], half)
        both = both[:tall] + both[tall:]
        blocks.append((both[:, :n], both[:, n:]))
    return blocks


def picks(shape, start, along):
    a = lax.broadcasted_iota(jnp.int32, shape, along)
    b = lax.broadcasted_iota(jnp.int32, shape, 1 - along)
    return jnp.where(a == b + start, 1.0, 0.0).astype(BF16)


def kernel(
    ox_ref,
    oy_ref,
    count_ref,
    contrast_hbm,
    probe_hbm,
    measured_hbm,
    rights_hbm,
    lefts_hbm,
    own_hbm,
    rim_hbm,
    contrast,
    measured,
    rights,
    lefts,
    ext,
    cut_rows,
    cut_columns,
    put_columns,
    put_rows,
    blocks,
    trans,
    waves,
    half,
    sent,
    landed,
    spread,
    rim_out,
    out,
    load,
    store,
    block_send,
    block_recv,
    grad_send,
    grad_recv,
    rim_send,
    rim_recv,
    back_send,
    back_recv,
    here,
    *,
    n_beam,
    n_lat,
):
    slots, n = measured_hbm.shape[0], measured_hbm.shape[1]
    wide = contrast_hbm.shape[3]
    stride = n_beam // slots
    me = lax.axis_index("beam")
    lat = lax.axis_index("lat")
    before, after = lat - 1, lat + 1
    has_before, has_after = lat > 0, lat < n_lat - 1

    def hosts(i):
        return lax.rem(i, stride) == 0

    def slot_of(i):
        return i // stride

    def host(j):
        return j * stride

    lower = jnp.where(hosts(me), me, (me + stride - 1) // stride)
    works = hosts(me)
    slot = slot_of(me)

    def meets(i, j):
        return hosts(i) | hosts(j)

    object_load = pltpu.make_async_copy(contrast_hbm, contrast, load.at[0])
    object_load.start()
    loads = [
        pltpu.make_async_copy(probe_hbm, waves.at[0], load.at[1]),
        pltpu.make_async_copy(rights_hbm, rights, load.at[2]),
        pltpu.make_async_copy(lefts_hbm, lefts, load.at[3]),
        pltpu.make_async_copy(measured_hbm.at[slot], measured, load.at[4]),
    ]

    barrier = pltpu.get_barrier_semaphore()
    for there, other in ((has_before, before), (has_after, after)):

        @pl.when(there)
        def _(other=other):
            pl.semaphore_signal(barrier, inc=1, device_id={"lat": other}, device_id_type=MESH)

    @pl.loop(me + 1, n_beam)
    def _(other):
        @pl.when(meets(me, other))
        def _():
            pl.semaphore_signal(barrier, inc=1, device_id={"beam": other}, device_id_type=MESH)

    object_load.wait()
    for part in (0, 1):
        ext[part, 0:n] = contrast[part, 0].astype(BF16)
    pl.semaphore_wait(barrier, lower + jnp.where(has_before & has_after, 2, 1))

    rims = [
        pltpu.make_async_remote_copy(
            src_ref=ext.at[part, 0:n],
            dst_ref=ext.at[part, n : 2 * n],
            send_sem=rim_send.at[part],
            recv_sem=rim_recv.at[part],
            device_id={"lat": before},
            device_id_type=MESH,
        )
        for part in (0, 1)
    ]

    @pl.when(has_before)
    def _():
        for rim in rims:
            rim.start()

    @pl.loop(0, me)
    def _(other):
        @pl.when(meets(me, other))
        def _():
            pl.semaphore_signal(here.at[me], inc=1, device_id={"beam": other}, device_id_type=MESH)

    @pl.when(works)
    def _():
        for copy in loads:
            copy.start()

    @pl.loop(0, slots)
    def _(j):
        x, y = ox_ref[j], oy_ref[j]
        cut_rows[j] = picks((n, 2 * n), x, 1)
        cut_columns[j] = picks((wide, n), y, 0)
        put_columns[j] = picks((n, wide), y, 1)
        put_rows[j, 0] = picks((n, n), x, 0)
        put_rows[j, 1] = picks((n, n), x - n, 0)

    def block_copy(j):
        return pltpu.make_async_remote_copy(
            src_ref=blocks.at[j],
            dst_ref=trans.at[me],
            send_sem=block_send.at[j],
            recv_sem=block_recv.at[me],
            device_id={"beam": host(j)},
            device_id_type=MESH,
        )

    group = 4
    for part in (0, 1):

        @pl.when(has_after)
        def _(part=part):
            rims[part].wait_recv()

        @pl.when(jnp.logical_not(has_after))
        def _(part=part):
            ext[part, n : 2 * n] = jnp.zeros((n, wide), BF16)

        @pl.loop(0, slots // group)
        def _(g, part=part):
            members = [g * group + m for m in range(group)]
            picked = [dot(cut_rows[j], ext[part]).astype(BF16) for j in members]
            picked = [dot(p, cut_columns[j]).astype(BF16) for p, j in zip(picked, members)]
            for p, j in zip(picked, members):
                blocks[j, part] = p
            if part == 1:
                for j in members:

                    @pl.when(host(j) < me)
                    def _(j=j):
                        block_copy(j).start()

                    @pl.when(host(j) == me)
                    def _(j=j):
                        pltpu.make_async_copy(blocks.at[j], trans.at[me], block_recv.at[me]).start()

    @pl.loop(me + 1, n_beam)
    def _(other):
        @pl.when(meets(me, other))
        def _():
            pl.semaphore_wait(here.at[other], 1)

            @pl.when(hosts(other))
            def _():
                block_copy(slot_of(other)).start()

    def grad_copy(k):
        return pltpu.make_async_remote_copy(
            src_ref=sent.at[k],
            dst_ref=landed.at[slot],
            send_sem=grad_send.at[k],
            recv_sem=grad_recv.at[slot],
            device_id={"beam": k},
            device_id_type=MESH,
        )

    tall = n // ROW_BLOCKS

    def times_trans(k, field):
        out = []
        for b, (re, im) in enumerate(field):
            rows = slice(b * tall, (b + 1) * tall)
            t_re = 1.0 + trans[k, 0, rows].astype(F32)
            t_im = trans[k, 1, rows].astype(F32)
            out.append((t_re * re - t_im * im, t_re * im + t_im * re))
        return out

    def wait_block(k):
        pltpu.make_async_copy(blocks.at[0], trans.at[k], block_recv.at[k]).wait()

    def keep(k, field):
        for b, (re, im) in enumerate(field):
            rows = slice(b * tall, (b + 1) * tall)
            waves[k, 0, rows] = re
            waves[k, 1, rows] = im

    def kept(k):
        return [
            (waves[k, 0, b * tall : (b + 1) * tall], waves[k, 1, b * tall : (b + 1) * tall])
            for b in range(ROW_BLOCKS)
        ]

    def give(k, field):
        for b, ((w_re, w_im), (d_re, d_im)) in enumerate(zip(kept(k), field)):
            rows = slice(b * tall, (b + 1) * tall)
            sent[k, 0, rows] = (w_re * d_re - w_im * d_im).astype(BF16)
            sent[k, 1, rows] = -(w_re * d_im + w_im * d_re).astype(BF16)

    def post(k):
        @pl.when(k != me)
        def _():
            grad_copy(k).start()

        @pl.when(k == me)
        def _():
            pltpu.make_async_copy(sent.at[k], landed.at[slot], grad_recv.at[slot]).start()

    @pl.when(works)
    def _():
        for copy in loads:
            copy.wait()
        wait_block(0)
        half[...] = by_right(times_trans(0, kept(0)), rights.at[0])

        @pl.loop(1, n_beam)
        def _(k):
            wait_block(k)
            field = by_left(lefts.at[0], half[...])
            keep(k, field)
            table = k // (n_beam - 1)
            half[...] = by_right(times_trans(k, field), rights.at[table])

        last = n_beam - 1
        live = jnp.where(slot < count_ref[0], 1.0, 0.0)
        field = []
        for b, (re, im) in enumerate(by_left(lefts.at[1], half[...])):
            misfit = live * (re * re + im * im - measured[b * tall : (b + 1) * tall])
            field.append((misfit * re, -(misfit * im)))
        half[...] = by_right(field, rights.at[1])

        @pl.loop(0, last)
        def _(i):
            k = last - i
            field = by_left(lefts.at[(k + 1) // n_beam], half[...])
            half[...] = by_right(times_trans(k, field), rights.at[0])
            give(k, field)
            post(k)

        give(0, by_left(lefts.at[0], half[...]))
        post(0)

    @pl.loop(0, slots)
    def _(j):
        pltpu.make_async_copy(sent.at[0], landed.at[j], grad_recv.at[j]).wait()
        both = jnp.concatenate([landed[j, 0], landed[j, 1]], axis=0)
        both = dot(both, put_columns[j]).astype(BF16)
        place = pl.ds(pl.multiple_of(j * n, n), n)
        spread[0, place] = both[0:n]
        spread[1, place] = both[n : 2 * n]

    def gathered(part, beyond):
        rows = jnp.concatenate([put_rows[j, beyond] for j in range(slots)], axis=1)
        return dot(rows, spread[part])

    backs = [
        pltpu.make_async_remote_copy(
            src_ref=rim_out.at[part],
            dst_ref=rim_hbm.at[part, 0],
            send_sem=back_send.at[part],
            recv_sem=back_recv.at[part],
            device_id={"lat": after},
            device_id_type=MESH,
        )
        for part in (0, 1)
    ]
    for part in (0, 1):
        rim_out[part] = gathered(part, 1).astype(BF16)

        @pl.when(has_after)
        def _(part=part):
            backs[part].start()

    for part in (0, 1):
        out[part, 0] = gathered(part, 0)
        pltpu.make_async_copy(out.at[part], own_hbm.at[part], store.at[part]).start()

    for part in (0, 1):
        pltpu.make_async_copy(out.at[part], own_hbm.at[part], store.at[part]).wait()

        @pl.when(has_before)
        def _(part=part):
            backs[part].wait_recv()

        @pl.when(has_before)
        def _(part=part):
            rims[part].wait_send()

        @pl.when(has_after)
        def _(part=part):
            backs[part].wait_send()

    @pl.loop(0, slots)
    def _(j):
        @pl.when(host(j) != me)
        def _():
            block_copy(j).wait_send()

    @pl.when(works)
    def _():
        @pl.loop(0, n_beam)
        def _(k):
            @pl.when(k != me)
            def _():
                grad_copy(k).wait_send()


def on_device(n_beam, n_lat, contrast, probe, offset_x, offset_y, probe_count, measured):
    slots, n = measured.shape[0], measured.shape[1]
    wide = contrast.shape[3]
    rights, lefts = host_tables(n)
    smem = pl.BlockSpec(memory_space=pltpu.SMEM)
    hbm = pl.BlockSpec(memory_space=pltpu.HBM)
    dma = pltpu.SemaphoreType.DMA
    own, rim = pl.pallas_call(
        functools.partial(kernel, n_beam=n_beam, n_lat=n_lat),
        out_shape=[
            jax.ShapeDtypeStruct(contrast.shape, F32),
            jax.ShapeDtypeStruct(contrast.shape, BF16),
        ],
        in_specs=[smem] * 3 + [hbm] * 5,
        out_specs=[hbm, hbm],
        scratch_shapes=[
            pltpu.VMEM(contrast.shape, F32),
            pltpu.VMEM((n, n), F32),
            pltpu.VMEM(rights.shape, BF16),
            pltpu.VMEM(lefts.shape, BF16),
            pltpu.VMEM((2, 2 * n, wide), BF16),
            pltpu.VMEM((slots, n, 2 * n), BF16),
            pltpu.VMEM((slots, wide, n), BF16),
            pltpu.VMEM((slots, n, wide), BF16),
            pltpu.VMEM((slots, 2, n, n), BF16),
            pltpu.VMEM((slots, 2, n, n), BF16),
            pltpu.VMEM((n_beam, 2, n, n), BF16),
            pltpu.VMEM((n_beam, 2, n, n), F32),
            pltpu.VMEM((2 * n, 2 * n), BF16),
            pltpu.VMEM((n_beam, 2, n, n), BF16),
            pltpu.VMEM((slots, 2, n, n), BF16),
            pltpu.VMEM((2, slots * n, wide), BF16),
            pltpu.VMEM((2, n, wide), BF16),
            pltpu.VMEM(contrast.shape, F32),
            dma((5,)),
            dma((2,)),
            dma((slots,)),
            dma((n_beam,)),
            dma((n_beam,)),
            dma((slots,)),
            dma((2,)),
            dma((2,)),
            dma((2,)),
            dma((2,)),
            pltpu.SemaphoreType.REGULAR((n_beam,)),
        ],
        compiler_params=pltpu.CompilerParams(
            collective_id=0, has_side_effects=True, vmem_limit_bytes=60 << 20
        ),
    )(offset_x, offset_y, probe_count, contrast, probe, measured, jnp.asarray(rights), jnp.asarray(lefts))
    return own + jnp.where(lax.axis_index("lat") > 0, rim.astype(F32), 0.0)


def solution(mesh):
    in_specs = (
        P(None, "beam", "lat", None),
        P(),
        P("lat"),
        P("lat"),
        P("lat"),
        P("lat", None, None),
    )
    return jax.shard_map(
        functools.partial(on_device, mesh.shape["beam"], mesh.shape["lat"]),
        mesh=mesh,
        in_specs=in_specs,
        out_specs=P(None, "beam", "lat", None),
        check_vma=False,
    )
```

```python
import functools
import math

import jax
import jax.numpy as jnp
import numpy as np
from jax import lax
from jax.experimental import pallas as pl
from jax.experimental.pallas import tpu as pltpu
from jax.sharding import PartitionSpec as P

MESH = pl.DeviceIdType.MESH
BF16 = jnp.bfloat16
F32 = jnp.float32
ROW_BLOCKS = 2
HOSTS = (0, 2, 4, 6, 8, 10, 12, 1)


def host_tables(order):
    index = np.arange(order)
    dft = np.exp(-2j * np.pi * (np.outer(index, index) % order) / order) / math.sqrt(order)
    shifted = (index + order // 2) % order - order // 2
    phase = np.exp(-1j * np.pi * (shifted * shifted) / (2 * order))
    step = dft.conj() @ (phase[:, None] * dft)

    def halves(form):
        high = form.astype(np.float32).astype(jnp.bfloat16)
        low = (form - high.astype(np.float64)).astype(np.float32).astype(jnp.bfloat16)
        return np.stack([high, low])

    rights, lefts = [], []
    for matrix in (step, dft):
        re, im = matrix.real, matrix.imag
        rights.append(halves(np.block([[re, im], [-im, re]])))
        rows = halves(np.block([re, im])).reshape(2, ROW_BLOCKS, order // ROW_BLOCKS, 2 * order)
        lefts.append(rows.transpose(1, 0, 2, 3).reshape(2 * order, 2 * order))
    return np.stack(rights), np.stack(lefts)


def dot(a, b):
    return jnp.dot(a, b, preferred_element_type=F32)


def by_right(blocks, right):
    halves = []
    for re, im in blocks:
        both = jnp.concatenate([re, im], axis=1).astype(BF16)
        halves.append(dot(both, right[0]) + dot(both, right[1]))
    half = jnp.concatenate(halves, axis=0)
    n = half.shape[0]
    turned = jnp.concatenate([-half[:, n:], half[:, :n]], axis=1)
    return jnp.concatenate([half.astype(BF16), turned.astype(BF16)], axis=0)


def by_left(left, half):
    blocks = []
    n = left.shape[1] // 2
    tall = n // ROW_BLOCKS
    for b in range(ROW_BLOCKS):
        both = dot(left[2 * b * tall : 2 * (b + 1) * tall], half)
        both = both[:tall] + both[tall:]
        blocks.append((both[:, :n], both[:, n:]))
    return blocks


def picks(shape, start, along):
    a = lax.broadcasted_iota(jnp.int32, shape, along)
    b = lax.broadcasted_iota(jnp.int32, shape, 1 - along)
    return jnp.where(a == b + start, 1.0, 0.0).astype(BF16)


def kernel(
    ox_ref,
    oy_ref,
    count_ref,
    contrast_hbm,
    probe_hbm,
    measured_hbm,
    rights_hbm,
    lefts_hbm,
    own_hbm,
    rim_hbm,
    contrast,
    measured,
    rights,
    lefts,
    ext,
    cut_rows,
    cut_columns,
    put_columns,
    put_rows,
    blocks,
    trans,
    waves,
    half,
    sent,
    landed,
    spread,
    rim_out,
    out,
    load,
    store,
    block_send,
    block_recv,
    grad_send,
    grad_recv,
    rim_send,
    rim_recv,
    back_send,
    back_recv,
    here,
    *,
    n_beam,
    n_lat,
):
    slots, n = measured_hbm.shape[0], measured_hbm.shape[1]
    wide = contrast_hbm.shape[3]
    me = lax.axis_index("beam")
    lat = lax.axis_index("lat")
    before, after = lat - 1, lat + 1
    has_before, has_after = lat > 0, lat < n_lat - 1

    def hosts(i):
        found = i == HOSTS[0]
        for h in HOSTS[1:]:
            found = found | (i == h)
        return found

    def slot_of(i):
        found = 0
        for j, h in enumerate(HOSTS):
            found = jnp.where(i == h, j, found)
        return found

    def host(j):
        found = HOSTS[0]
        for other, h in enumerate(HOSTS):
            found = jnp.where(j == other, h, found)
        return found

    below = 0
    for h in HOSTS:
        below = below + jnp.where(h < me, 1, 0)
    lower = jnp.where(hosts(me), me, below)
    works = hosts(me)
    slot = slot_of(me)

    def meets(i, j):
        return hosts(i) | hosts(j)

    object_load = pltpu.make_async_copy(contrast_hbm, contrast, load.at[0])
    object_load.start()
    loads = [
        pltpu.make_async_copy(probe_hbm, waves.at[0], load.at[1]),
        pltpu.make_async_copy(rights_hbm, rights, load.at[2]),
        pltpu.make_async_copy(lefts_hbm, lefts, load.at[3]),
        pltpu.make_async_copy(measured_hbm.at[slot], measured, load.at[4]),
    ]

    barrier = pltpu.get_barrier_semaphore()
    for there, other in ((has_before, before), (has_after, after)):

        @pl.when(there)
        def _(other=other):
            pl.semaphore_signal(barrier, inc=1, device_id={"lat": other}, device_id_type=MESH)

    @pl.loop(me + 1, n_beam)
    def _(other):
        @pl.when(meets(me, other))
        def _():
            pl.semaphore_signal(barrier, inc=1, device_id={"beam": other}, device_id_type=MESH)

    object_load.wait()
    for part in (0, 1):
        ext[part, 0:n] = contrast[part, 0].astype(BF16)
    pl.semaphore_wait(barrier, lower + jnp.where(has_before & has_after, 2, 1))

    low = n // 2
    rims = [
        pltpu.make_async_remote_copy(
            src_ref=ext.at[:, h * low : (h + 1) * low],
            dst_ref=ext.at[:, n + h * low : n + (h + 1) * low],
            send_sem=rim_send.at[h],
            recv_sem=rim_recv.at[h],
            device_id={"lat": before},
            device_id_type=MESH,
        )
        for h in (0, 1)
    ]

    @pl.when(has_before)
    def _():
        for rim in rims:
            rim.start()

    @pl.loop(0, me)
    def _(other):
        @pl.when(meets(me, other))
        def _():
            pl.semaphore_signal(here.at[me], inc=1, device_id={"beam": other}, device_id_type=MESH)

    @pl.when(works)
    def _():
        for copy in loads:
            copy.start()

    @pl.loop(0, slots)
    def _(j):
        x, y = ox_ref[j], oy_ref[j]
        cut_rows[j] = picks((low, low + n), x, 1)
        cut_columns[j] = picks((wide, n), y, 0)
        put_columns[j] = picks((n, wide), y, 1)
        put_rows[j, 0] = picks((n, n), x, 0)
        put_rows[j, 1] = picks((n, n), x - n, 0)

    def block_copy(j):
        return pltpu.make_async_remote_copy(
            src_ref=blocks.at[j],
            dst_ref=trans.at[me],
            send_sem=block_send.at[j],
            recv_sem=block_recv.at[me],
            device_id={"beam": host(j)},
            device_id_type=MESH,
        )

    def half_copy(j, h):
        rows = slice(h * low, (h + 1) * low)
        return pltpu.make_async_remote_copy(
            src_ref=blocks.at[j, :, rows],
            dst_ref=trans.at[me, :, rows],
            send_sem=block_send.at[j],
            recv_sem=block_recv.at[me],
            device_id={"beam": host(j)},
            device_id_type=MESH,
        )

    group = 4
    for h in (0, 1):
        rows = slice(h * low, (h + 1) * low)

        @pl.when(has_after)
        def _(h=h):
            rims[h].wait_recv()

        @pl.when(jnp.logical_not(has_after))
        def _(h=h):
            ext[:, n + h * low : n + (h + 1) * low] = jnp.zeros((2, low, wide), BF16)

        @pl.loop(0, slots // group)
        def _(g, h=h, rows=rows):
            members = [g * group + m for m in range(group)]
            lines = jnp.concatenate([cut_rows[j] for j in members], axis=0)
            picked = [
                dot(lines, ext[part, h * low : h * low + low + n]).astype(BF16) for part in (0, 1)
            ]
            for m, j in enumerate(members):
                own = slice(m * low, (m + 1) * low)
                both = jnp.concatenate([picked[0][own], picked[1][own]], axis=0)
                both = dot(both, cut_columns[j]).astype(BF16)
                blocks[j, 0, rows] = both[:low]
                blocks[j, 1, rows] = both[low:]
            for j in members:

                @pl.when(host(j) < me)
                def _(j=j):
                    half_copy(j, h).start()

                if h == 1:

                    @pl.when(host(j) == me)
                    def _(j=j):
                        pltpu.make_async_copy(blocks.at[j], trans.at[me], block_recv.at[me]).start()

    @pl.loop(me + 1, n_beam)
    def _(other):
        @pl.when(meets(me, other))
        def _():
            pl.semaphore_wait(here.at[other], 1)

            @pl.when(hosts(other))
            def _():
                block_copy(slot_of(other)).start()

    def grad_copy(k):
        return pltpu.make_async_remote_copy(
            src_ref=sent.at[k],
            dst_ref=landed.at[slot],
            send_sem=grad_send.at[k],
            recv_sem=grad_recv.at[slot],
            device_id={"beam": k},
            device_id_type=MESH,
        )

    tall = n // ROW_BLOCKS

    def times_trans(k, field):
        out = []
        for b, (re, im) in enumerate(field):
            rows = slice(b * tall, (b + 1) * tall)
            t_re = 1.0 + trans[k, 0, rows].astype(F32)
            t_im = trans[k, 1, rows].astype(F32)
            out.append((t_re * re - t_im * im, t_re * im + t_im * re))
        return out

    def wait_block(k):
        pltpu.make_async_copy(blocks.at[0], trans.at[k], block_recv.at[k]).wait()

    def keep(k, field):
        for b, (re, im) in enumerate(field):
            rows = slice(b * tall, (b + 1) * tall)
            waves[k, 0, rows] = re
            waves[k, 1, rows] = im

    def kept(k):
        return [
            (waves[k, 0, b * tall : (b + 1) * tall], waves[k, 1, b * tall : (b + 1) * tall])
            for b in range(ROW_BLOCKS)
        ]

    def give(k, field):
        for b, ((w_re, w_im), (d_re, d_im)) in enumerate(zip(kept(k), field)):
            rows = slice(b * tall, (b + 1) * tall)
            sent[k, 0, rows] = (w_re * d_re - w_im * d_im).astype(BF16)
            sent[k, 1, rows] = -(w_re * d_im + w_im * d_re).astype(BF16)

    def post(k):
        @pl.when(k != me)
        def _():
            grad_copy(k).start()

        @pl.when(k == me)
        def _():
            pltpu.make_async_copy(sent.at[k], landed.at[slot], grad_recv.at[slot]).start()

    @pl.when(works)
    def _():
        for copy in loads:
            copy.wait()
        wait_block(0)
        half[...] = by_right(times_trans(0, kept(0)), rights.at[0])

        @pl.loop(1, n_beam)
        def _(k):
            wait_block(k)
            field = by_left(lefts.at[0], half[...])
            keep(k, field)
            table = k // (n_beam - 1)
            half[...] = by_right(times_trans(k, field), rights.at[table])

        last = n_beam - 1
        live = jnp.where(slot < count_ref[0], 1.0, 0.0)
        field = []
        for b, (re, im) in enumerate(by_left(lefts.at[1], half[...])):
            misfit = live * (re * re + im * im - measured[b * tall : (b + 1) * tall])
            field.append((misfit * re, -(misfit * im)))
        half[...] = by_right(field, rights.at[1])

        @pl.loop(0, last)
        def _(i):
            k = last - i
            field = by_left(lefts.at[(k + 1) // n_beam], half[...])
            half[...] = by_right(times_trans(k, field), rights.at[0])
            give(k, field)
            post(k)

        give(0, by_left(lefts.at[0], half[...]))
        post(0)

    @pl.loop(0, slots)
    def _(j):
        pltpu.make_async_copy(sent.at[0], landed.at[j], grad_recv.at[j]).wait()
        both = jnp.concatenate([landed[j, 0], landed[j, 1]], axis=0)
        both = dot(both, put_columns[j]).astype(BF16)
        place = pl.ds(pl.multiple_of(j * n, n), n)
        spread[0, place] = both[0:n]
        spread[1, place] = both[n : 2 * n]

    def gathered(part, beyond):
        rows = jnp.concatenate([put_rows[j, beyond] for j in range(slots)], axis=1)
        return dot(rows, spread[part])

    backs = [
        pltpu.make_async_remote_copy(
            src_ref=rim_out.at[part],
            dst_ref=rim_hbm.at[part, 0],
            send_sem=back_send.at[part],
            recv_sem=back_recv.at[part],
            device_id={"lat": after},
            device_id_type=MESH,
        )
        for part in (0, 1)
    ]
    for part in (0, 1):
        rim_out[part] = gathered(part, 1).astype(BF16)

        @pl.when(has_after)
        def _(part=part):
            backs[part].start()

    for part in (0, 1):
        out[part, 0] = gathered(part, 0)
        pltpu.make_async_copy(out.at[part], own_hbm.at[part], store.at[part]).start()

    for part in (0, 1):
        pltpu.make_async_copy(out.at[part], own_hbm.at[part], store.at[part]).wait()

        @pl.when(has_before)
        def _(part=part):
            backs[part].wait_recv()

        @pl.when(has_before)
        def _(part=part):
            rims[part].wait_send()

        @pl.when(has_after)
        def _(part=part):
            backs[part].wait_send()

    @pl.loop(0, slots)
    def _(j):
        @pl.when(host(j) != me)
        def _():
            block_copy(j).wait_send()

    @pl.when(works)
    def _():
        @pl.loop(0, n_beam)
        def _(k):
            @pl.when(k != me)
            def _():
                grad_copy(k).wait_send()


def on_device(n_beam, n_lat, contrast, probe, offset_x, offset_y, probe_count, measured):
    slots, n = measured.shape[0], measured.shape[1]
    wide = contrast.shape[3]
    rights, lefts = host_tables(n)
    smem = pl.BlockSpec(memory_space=pltpu.SMEM)
    hbm = pl.BlockSpec(memory_space=pltpu.HBM)
    dma = pltpu.SemaphoreType.DMA
    own, rim = pl.pallas_call(
        functools.partial(kernel, n_beam=n_beam, n_lat=n_lat),
        out_shape=[
            jax.ShapeDtypeStruct(contrast.shape, F32),
            jax.ShapeDtypeStruct(contrast.shape, BF16),
        ],
        in_specs=[smem] * 3 + [hbm] * 5,
        out_specs=[hbm, hbm],
        scratch_shapes=[
            pltpu.VMEM(contrast.shape, F32),
            pltpu.VMEM((n, n), F32),
            pltpu.VMEM(rights.shape, BF16),
            pltpu.VMEM(lefts.shape, BF16),
            pltpu.VMEM((2, 2 * n, wide), BF16),
            pltpu.VMEM((slots, n // 2, n // 2 + n), BF16),
            pltpu.VMEM((slots, wide, n), BF16),
            pltpu.VMEM((slots, n, wide), BF16),
            pltpu.VMEM((slots, 2, n, n), BF16),
            pltpu.VMEM((slots, 2, n, n), BF16),
            pltpu.VMEM((n_beam, 2, n, n), BF16),
            pltpu.VMEM((n_beam, 2, n, n), F32),
            pltpu.VMEM((2 * n, 2 * n), BF16),
            pltpu.VMEM((n_beam, 2, n, n), BF16),
            pltpu.VMEM((slots, 2, n, n), BF16),
            pltpu.VMEM((2, slots * n, wide), BF16),
            pltpu.VMEM((2, n, wide), BF16),
            pltpu.VMEM(contrast.shape, F32),
            dma((5,)),
            dma((2,)),
            dma((slots,)),
            dma((n_beam,)),
            dma((n_beam,)),
            dma((slots,)),
            dma((2,)),
            dma((2,)),
            dma((2,)),
            dma((2,)),
            pltpu.SemaphoreType.REGULAR((n_beam,)),
        ],
        compiler_params=pltpu.CompilerParams(
            collective_id=0, has_side_effects=True, vmem_limit_bytes=60 << 20
        ),
    )(offset_x, offset_y, probe_count, contrast, probe, measured, jnp.asarray(rights), jnp.asarray(lefts))
    return own + jnp.where(lax.axis_index("lat") > 0, rim.astype(F32), 0.0)


def solution(mesh):
    in_specs = (
        P(None, "beam", "lat", None),
        P(),
        P("lat"),
        P("lat"),
        P("lat"),
        P("lat", None, None),
    )
    return jax.shard_map(
        functools.partial(on_device, mesh.shape["beam"], mesh.shape["lat"]),
        mesh=mesh,
        in_specs=in_specs,
        out_specs=P(None, "beam", "lat", None),
        check_vma=False,
    )
```

```python
import functools
import math

import jax
import jax.numpy as jnp
import numpy as np
from jax import lax
from jax.experimental import pallas as pl
from jax.experimental.pallas import tpu as pltpu
from jax.sharding import PartitionSpec as P

MESH = pl.DeviceIdType.MESH
BF16 = jnp.bfloat16
F32 = jnp.float32
ROW_BLOCKS = 2
HOSTS = (0, 2, 4, 6, 8, 10, 12, 1)


def host_tables(order):
    index = np.arange(order)
    dft = np.exp(-2j * np.pi * (np.outer(index, index) % order) / order) / math.sqrt(order)
    shifted = (index + order // 2) % order - order // 2
    phase = np.exp(-1j * np.pi * (shifted * shifted) / (2 * order))
    step = dft.conj() @ (phase[:, None] * dft)

    def halves(form):
        high = form.astype(np.float32).astype(jnp.bfloat16)
        low = (form - high.astype(np.float64)).astype(np.float32).astype(jnp.bfloat16)
        return np.stack([high, low])

    rights, lefts = [], []
    for matrix in (step, dft):
        re, im = matrix.real, matrix.imag
        rights.append(halves(np.block([[re, im], [-im, re]])))
        rows = halves(np.block([re, im])).reshape(2, ROW_BLOCKS, order // ROW_BLOCKS, 2 * order)
        lefts.append(rows.transpose(1, 0, 2, 3).reshape(2 * order, 2 * order))
    return np.stack(rights), np.stack(lefts)


def dot(a, b):
    return jnp.dot(a, b, preferred_element_type=F32)


def by_right(blocks, right):
    halves = []
    for re, im in blocks:
        both = jnp.concatenate([re, im], axis=1).astype(BF16)
        halves.append(dot(both, right[0]) + dot(both, right[1]))
    half = jnp.concatenate(halves, axis=0)
    n = half.shape[0]
    turned = jnp.concatenate([-half[:, n:], half[:, :n]], axis=1)
    return jnp.concatenate([half.astype(BF16), turned.astype(BF16)], axis=0)


def by_left(left, half):
    blocks = []
    n = left.shape[1] // 2
    tall = n // ROW_BLOCKS
    for b in range(ROW_BLOCKS):
        both = dot(left[2 * b * tall : 2 * (b + 1) * tall], half)
        both = both[:tall] + both[tall:]
        blocks.append((both[:, :n], both[:, n:]))
    return blocks


def picks(shape, start, along):
    a = lax.broadcasted_iota(jnp.int32, shape, along)
    b = lax.broadcasted_iota(jnp.int32, shape, 1 - along)
    return jnp.where(a == b + start, 1.0, 0.0).astype(BF16)


def kernel(
    ox_ref,
    oy_ref,
    count_ref,
    contrast_hbm,
    probe_hbm,
    measured_hbm,
    rights_hbm,
    lefts_hbm,
    own_hbm,
    rim_hbm,
    contrast,
    measured,
    rights,
    lefts,
    ext,
    cut_rows,
    cut_columns,
    put_columns,
    put_rows,
    blocks,
    trans,
    waves,
    half,
    sent,
    landed,
    spread,
    rim_out,
    out,
    load,
    store,
    block_send,
    block_recv,
    grad_send,
    grad_recv,
    rim_send,
    rim_recv,
    back_send,
    back_recv,
    here,
    *,
    n_beam,
    n_lat,
):
    slots, n = measured_hbm.shape[0], measured_hbm.shape[1]
    wide = contrast_hbm.shape[3]
    me = lax.axis_index("beam")
    lat = lax.axis_index("lat")
    before, after = lat - 1, lat + 1
    has_before, has_after = lat > 0, lat < n_lat - 1

    def hosts(i):
        found = i == HOSTS[0]
        for h in HOSTS[1:]:
            found = found | (i == h)
        return found

    def slot_of(i):
        found = 0
        for j, h in enumerate(HOSTS):
            found = jnp.where(i == h, j, found)
        return found

    def host(j):
        found = HOSTS[0]
        for other, h in enumerate(HOSTS):
            found = jnp.where(j == other, h, found)
        return found

    below = 0
    for h in HOSTS:
        below = below + jnp.where(h < me, 1, 0)
    lower = jnp.where(hosts(me), me, below)
    works = hosts(me)
    slot = slot_of(me)

    def meets(i, j):
        return hosts(i) | hosts(j)

    object_load = pltpu.make_async_copy(contrast_hbm, contrast, load.at[0])
    object_load.start()
    loads = [
        pltpu.make_async_copy(probe_hbm, waves.at[0], load.at[1]),
        pltpu.make_async_copy(rights_hbm, rights, load.at[2]),
        pltpu.make_async_copy(lefts_hbm, lefts, load.at[3]),
        pltpu.make_async_copy(measured_hbm.at[slot], measured, load.at[4]),
    ]

    barrier = pltpu.get_barrier_semaphore()
    for there, other in ((has_before, before), (has_after, after)):

        @pl.when(there)
        def _(other=other):
            pl.semaphore_signal(barrier, inc=1, device_id={"lat": other}, device_id_type=MESH)

    @pl.loop(me + 1, n_beam)
    def _(other):
        @pl.when(meets(me, other))
        def _():
            pl.semaphore_signal(barrier, inc=1, device_id={"beam": other}, device_id_type=MESH)

    object_load.wait()
    for part in (0, 1):
        ext[part, 0:n] = contrast[part, 0].astype(BF16)
    pl.semaphore_wait(barrier, lower + jnp.where(has_before & has_after, 2, 1))

    low = n // 2
    rims = [
        pltpu.make_async_remote_copy(
            src_ref=ext.at[:, h * low : (h + 1) * low],
            dst_ref=ext.at[:, n + h * low : n + (h + 1) * low],
            send_sem=rim_send.at[h],
            recv_sem=rim_recv.at[h],
            device_id={"lat": before},
            device_id_type=MESH,
        )
        for h in (0, 1)
    ]

    @pl.loop(0, me)
    def _(other):
        @pl.when(meets(me, other))
        def _():
            pl.semaphore_signal(here.at[me], inc=1, device_id={"beam": other}, device_id_type=MESH)

    @pl.when(has_before)
    def _():
        for rim in rims:
            rim.start()

    @pl.when(works)
    def _():
        for copy in loads:
            copy.start()

    @pl.loop(0, slots)
    def _(j):
        x, y = ox_ref[j], oy_ref[j]
        cut_rows[j] = picks((low, low + n), x, 1)
        cut_columns[j] = picks((wide, n), y, 0)
        put_columns[j] = picks((n, wide), y, 1)
        put_rows[j, 0] = picks((n, n), x, 0)
        put_rows[j, 1] = picks((n, n), x - n, 0)

    def block_copy(j):
        return pltpu.make_async_remote_copy(
            src_ref=blocks.at[j],
            dst_ref=trans.at[me],
            send_sem=block_send.at[j],
            recv_sem=block_recv.at[me],
            device_id={"beam": host(j)},
            device_id_type=MESH,
        )

    def half_copy(j, h):
        rows = slice(h * low, (h + 1) * low)
        return pltpu.make_async_remote_copy(
            src_ref=blocks.at[j, :, rows],
            dst_ref=trans.at[me, :, rows],
            send_sem=block_send.at[j],
            recv_sem=block_recv.at[me],
            device_id={"beam": host(j)},
            device_id_type=MESH,
        )

    group = 4
    for h in (0, 1):
        rows = slice(h * low, (h + 1) * low)

        @pl.when(has_after)
        def _(h=h):
            rims[h].wait_recv()

        @pl.when(jnp.logical_not(has_after))
        def _(h=h):
            ext[:, n + h * low : n + (h + 1) * low] = jnp.zeros((2, low, wide), BF16)

        @pl.loop(0, slots // group)
        def _(g, h=h, rows=rows):
            members = [g * group + m for m in range(group)]
            lines = jnp.concatenate([cut_rows[j] for j in members], axis=0)
            picked = [
                dot(lines, ext[part, h * low : h * low + low + n]).astype(BF16) for part in (0, 1)
            ]
            for m, j in enumerate(members):
                own = slice(m * low, (m + 1) * low)
                both = jnp.concatenate([picked[0][own], picked[1][own]], axis=0)
                both = dot(both, cut_columns[j]).astype(BF16)
                blocks[j, 0, rows] = both[:low]
                blocks[j, 1, rows] = both[low:]
            for j in members:

                @pl.when(host(j) < me)
                def _(j=j):
                    half_copy(j, h).start()

                if h == 1:

                    @pl.when(host(j) == me)
                    def _(j=j):
                        pltpu.make_async_copy(blocks.at[j], trans.at[me], block_recv.at[me]).start()

    @pl.loop(me + 1, n_beam)
    def _(other):
        @pl.when(meets(me, other))
        def _():
            pl.semaphore_wait(here.at[other], 1)

            @pl.when(hosts(other))
            def _():
                block_copy(slot_of(other)).start()

    def grad_copy(k):
        return pltpu.make_async_remote_copy(
            src_ref=sent.at[k],
            dst_ref=landed.at[slot],
            send_sem=grad_send.at[k],
            recv_sem=grad_recv.at[slot],
            device_id={"beam": k},
            device_id_type=MESH,
        )

    tall = n // ROW_BLOCKS

    def times_trans(k, field):
        out = []
        for b, (re, im) in enumerate(field):
            rows = slice(b * tall, (b + 1) * tall)
            t_re = 1.0 + trans[k, 0, rows].astype(F32)
            t_im = trans[k, 1, rows].astype(F32)
            out.append((t_re * re - t_im * im, t_re * im + t_im * re))
        return out

    def wait_block(k):
        pltpu.make_async_copy(blocks.at[0], trans.at[k], block_recv.at[k]).wait()

    def keep(k, field):
        for b, (re, im) in enumerate(field):
            rows = slice(b * tall, (b + 1) * tall)
            waves[k, 0, rows] = re
            waves[k, 1, rows] = im

    def kept(k):
        return [
            (waves[k, 0, b * tall : (b + 1) * tall], waves[k, 1, b * tall : (b + 1) * tall])
            for b in range(ROW_BLOCKS)
        ]

    def give(k, field):
        for b, ((w_re, w_im), (d_re, d_im)) in enumerate(zip(kept(k), field)):
            rows = slice(b * tall, (b + 1) * tall)
            sent[k, 0, rows] = (w_re * d_re - w_im * d_im).astype(BF16)
            sent[k, 1, rows] = -(w_re * d_im + w_im * d_re).astype(BF16)

    def post(k):
        @pl.when(k != me)
        def _():
            grad_copy(k).start()

        @pl.when(k == me)
        def _():
            pltpu.make_async_copy(sent.at[k], landed.at[slot], grad_recv.at[slot]).start()

    @pl.when(works)
    def _():
        for copy in loads:
            copy.wait()
        wait_block(0)
        half[...] = by_right(times_trans(0, kept(0)), rights.at[0])

        @pl.loop(1, n_beam)
        def _(k):
            wait_block(k)
            field = by_left(lefts.at[0], half[...])
            keep(k, field)
            table = k // (n_beam - 1)
            half[...] = by_right(times_trans(k, field), rights.at[table])

        last = n_beam - 1
        live = jnp.where(slot < count_ref[0], 1.0, 0.0)
        field = []
        for b, (re, im) in enumerate(by_left(lefts.at[1], half[...])):
            misfit = live * (re * re + im * im - measured[b * tall : (b + 1) * tall])
            field.append((misfit * re, -(misfit * im)))
        half[...] = by_right(field, rights.at[1])

        @pl.loop(0, last)
        def _(i):
            k = last - i
            field = by_left(lefts.at[(k + 1) // n_beam], half[...])
            half[...] = by_right(times_trans(k, field), rights.at[0])
            give(k, field)
            post(k)

        give(0, by_left(lefts.at[0], half[...]))
        post(0)

    @pl.loop(0, slots)
    def _(j):
        pltpu.make_async_copy(sent.at[0], landed.at[j], grad_recv.at[j]).wait()
        both = jnp.concatenate([landed[j, 0], landed[j, 1]], axis=0)
        both = dot(both, put_columns[j]).astype(BF16)
        place = pl.ds(pl.multiple_of(j * n, n), n)
        spread[0, place] = both[0:n]
        spread[1, place] = both[n : 2 * n]

    def gathered(part, beyond):
        rows = jnp.concatenate([put_rows[j, beyond] for j in range(slots)], axis=1)
        return dot(rows, spread[part])

    backs = [
        pltpu.make_async_remote_copy(
            src_ref=rim_out.at[part],
            dst_ref=rim_hbm.at[part, 0],
            send_sem=back_send.at[part],
            recv_sem=back_recv.at[part],
            device_id={"lat": after},
            device_id_type=MESH,
        )
        for part in (0, 1)
    ]
    for part in (0, 1):
        rim_out[part] = gathered(part, 1).astype(BF16)

        @pl.when(has_after)
        def _(part=part):
            backs[part].start()

    for part in (0, 1):
        out[part, 0] = gathered(part, 0)
        pltpu.make_async_copy(out.at[part], own_hbm.at[part], store.at[part]).start()

    for part in (0, 1):
        pltpu.make_async_copy(out.at[part], own_hbm.at[part], store.at[part]).wait()

        @pl.when(has_before)
        def _(part=part):
            backs[part].wait_recv()

        @pl.when(has_before)
        def _(part=part):
            rims[part].wait_send()

        @pl.when(has_after)
        def _(part=part):
            backs[part].wait_send()

    @pl.loop(0, slots)
    def _(j):
        @pl.when(host(j) != me)
        def _():
            block_copy(j).wait_send()

    @pl.when(works)
    def _():
        @pl.loop(0, n_beam)
        def _(k):
            @pl.when(k != me)
            def _():
                grad_copy(k).wait_send()


def on_device(n_beam, n_lat, contrast, probe, offset_x, offset_y, probe_count, measured):
    slots, n = measured.shape[0], measured.shape[1]
    wide = contrast.shape[3]
    rights, lefts = host_tables(n)
    smem = pl.BlockSpec(memory_space=pltpu.SMEM)
    hbm = pl.BlockSpec(memory_space=pltpu.HBM)
    dma = pltpu.SemaphoreType.DMA
    own, rim = pl.pallas_call(
        functools.partial(kernel, n_beam=n_beam, n_lat=n_lat),
        out_shape=[
            jax.ShapeDtypeStruct(contrast.shape, F32),
            jax.ShapeDtypeStruct(contrast.shape, BF16),
        ],
        in_specs=[smem] * 3 + [hbm] * 5,
        out_specs=[hbm, hbm],
        scratch_shapes=[
            pltpu.VMEM(contrast.shape, F32),
            pltpu.VMEM((n, n), F32),
            pltpu.VMEM(rights.shape, BF16),
            pltpu.VMEM(lefts.shape, BF16),
            pltpu.VMEM((2, 2 * n, wide), BF16),
            pltpu.VMEM((slots, n // 2, n // 2 + n), BF16),
            pltpu.VMEM((slots, wide, n), BF16),
            pltpu.VMEM((slots, n, wide), BF16),
            pltpu.VMEM((slots, 2, n, n), BF16),
            pltpu.VMEM((slots, 2, n, n), BF16),
            pltpu.VMEM((n_beam, 2, n, n), BF16),
            pltpu.VMEM((n_beam, 2, n, n), F32),
            pltpu.VMEM((2 * n, 2 * n), BF16),
            pltpu.VMEM((n_beam, 2, n, n), BF16),
            pltpu.VMEM((slots, 2, n, n), BF16),
            pltpu.VMEM((2, slots * n, wide), BF16),
            pltpu.VMEM((2, n, wide), BF16),
            pltpu.VMEM(contrast.shape, F32),
            dma((5,)),
            dma((2,)),
            dma((slots,)),
            dma((n_beam,)),
            dma((n_beam,)),
            dma((slots,)),
            dma((2,)),
            dma((2,)),
            dma((2,)),
            dma((2,)),
            pltpu.SemaphoreType.REGULAR((n_beam,)),
        ],
        compiler_params=pltpu.CompilerParams(
            collective_id=0, has_side_effects=True, vmem_limit_bytes=60 << 20
        ),
    )(offset_x, offset_y, probe_count, contrast, probe, measured, jnp.asarray(rights), jnp.asarray(lefts))
    return own + jnp.where(lax.axis_index("lat") > 0, rim.astype(F32), 0.0)


def solution(mesh):
    in_specs = (
        P(None, "beam", "lat", None),
        P(),
        P("lat"),
        P("lat"),
        P("lat"),
        P("lat", None, None),
    )
    return jax.shard_map(
        functools.partial(on_device, mesh.shape["beam"], mesh.shape["lat"]),
        mesh=mesh,
        in_specs=in_specs,
        out_specs=P(None, "beam", "lat", None),
        check_vma=False,
    )
```

```python
import functools
import math

import jax
import jax.numpy as jnp
import numpy as np
from jax import lax
from jax.experimental import pallas as pl
from jax.experimental.pallas import tpu as pltpu
from jax.sharding import PartitionSpec as P

MESH = pl.DeviceIdType.MESH
BF16 = jnp.bfloat16
F32 = jnp.float32
ROW_BLOCKS = 2
HOSTS = (0, 2, 4, 6, 8, 10, 12, 1)


def host_tables(order):
    index = np.arange(order)
    dft = np.exp(-2j * np.pi * (np.outer(index, index) % order) / order) / math.sqrt(order)
    shifted = (index + order // 2) % order - order // 2
    phase = np.exp(-1j * np.pi * (shifted * shifted) / (2 * order))
    step = dft.conj() @ (phase[:, None] * dft)

    def halves(form):
        high = form.astype(np.float32).astype(jnp.bfloat16)
        low = (form - high.astype(np.float64)).astype(np.float32).astype(jnp.bfloat16)
        return np.stack([high, low])

    rights, lefts = [], []
    for matrix in (step, dft):
        re, im = matrix.real, matrix.imag
        rights.append(halves(np.block([[re, im], [-im, re]])))
        rows = halves(np.block([re, im])).reshape(2, ROW_BLOCKS, order // ROW_BLOCKS, 2 * order)
        lefts.append(rows.transpose(1, 0, 2, 3).reshape(2 * order, 2 * order))
    return np.stack(rights), np.stack(lefts)


def dot(a, b):
    return jnp.dot(a, b, preferred_element_type=F32)


def by_right(blocks, right):
    halves = []
    for re, im in blocks:
        both = jnp.concatenate([re, im], axis=1).astype(BF16)
        halves.append(dot(both, right[0]) + dot(both, right[1]))
    half = jnp.concatenate(halves, axis=0)
    n = half.shape[0]
    turned = jnp.concatenate([-half[:, n:], half[:, :n]], axis=1)
    return jnp.concatenate([half.astype(BF16), turned.astype(BF16)], axis=0)


def by_left(left, half):
    blocks = []
    n = left.shape[1] // 2
    tall = n // ROW_BLOCKS
    for b in range(ROW_BLOCKS):
        both = dot(left[2 * b * tall : 2 * (b + 1) * tall], half)
        both = both[:tall] + both[tall:]
        blocks.append((both[:, :n], both[:, n:]))
    return blocks


def picks(shape, start, along):
    a = lax.broadcasted_iota(jnp.int32, shape, along)
    b = lax.broadcasted_iota(jnp.int32, shape, 1 - along)
    return jnp.where(a == b + start, 1.0, 0.0).astype(BF16)


def kernel(
    ox_ref,
    oy_ref,
    count_ref,
    contrast_hbm,
    probe_hbm,
    measured_hbm,
    rights_hbm,
    lefts_hbm,
    own_hbm,
    rim_hbm,
    contrast,
    measured,
    rights,
    lefts,
    ext,
    cut_rows,
    cut_columns,
    put_columns,
    put_rows,
    blocks,
    trans,
    waves,
    half,
    sent,
    landed,
    spread,
    rim_out,
    out,
    load,
    store,
    block_send,
    block_recv,
    grad_send,
    grad_recv,
    rim_send,
    rim_recv,
    back_send,
    back_recv,
    here,
    *,
    n_beam,
    n_lat,
):
    slots, n = measured_hbm.shape[0], measured_hbm.shape[1]
    wide = contrast_hbm.shape[3]
    me = lax.axis_index("beam")
    lat = lax.axis_index("lat")
    before, after = lat - 1, lat + 1
    has_before, has_after = lat > 0, lat < n_lat - 1

    def hosts(i):
        found = i == HOSTS[0]
        for h in HOSTS[1:]:
            found = found | (i == h)
        return found

    def slot_of(i):
        found = 0
        for j, h in enumerate(HOSTS):
            found = jnp.where(i == h, j, found)
        return found

    def host(j):
        found = HOSTS[0]
        for other, h in enumerate(HOSTS):
            found = jnp.where(j == other, h, found)
        return found

    below = 0
    for h in HOSTS:
        below = below + jnp.where(h < me, 1, 0)
    lower = jnp.where(hosts(me), me, below)
    works = hosts(me)
    slot = slot_of(me)

    def meets(i, j):
        return hosts(i) | hosts(j)

    object_load = pltpu.make_async_copy(contrast_hbm, contrast, load.at[0])
    object_load.start()
    loads = [
        pltpu.make_async_copy(probe_hbm, waves.at[0], load.at[1]),
        pltpu.make_async_copy(rights_hbm, rights, load.at[2]),
        pltpu.make_async_copy(lefts_hbm, lefts, load.at[3]),
        pltpu.make_async_copy(measured_hbm.at[slot], measured, load.at[4]),
    ]

    barrier = pltpu.get_barrier_semaphore()
    for there, other in ((has_before, before), (has_after, after)):

        @pl.when(there)
        def _(other=other):
            pl.semaphore_signal(barrier, inc=1, device_id={"lat": other}, device_id_type=MESH)

    @pl.loop(me + 1, n_beam)
    def _(other):
        @pl.when(meets(me, other))
        def _():
            pl.semaphore_signal(barrier, inc=1, device_id={"beam": other}, device_id_type=MESH)

    object_load.wait()
    for part in (0, 1):
        ext[part, 0:n] = contrast[part, 0].astype(BF16)
    pl.semaphore_wait(barrier, lower + jnp.where(has_before & has_after, 2, 1))

    low = n // 2
    rims = [
        pltpu.make_async_remote_copy(
            src_ref=ext.at[:, h * low : (h + 1) * low],
            dst_ref=ext.at[:, n + h * low : n + (h + 1) * low],
            send_sem=rim_send.at[h],
            recv_sem=rim_recv.at[h],
            device_id={"lat": before},
            device_id_type=MESH,
        )
        for h in (0, 1)
    ]

    @pl.loop(0, me)
    def _(other):
        @pl.when(meets(me, other))
        def _():
            pl.semaphore_signal(here.at[me], inc=1, device_id={"beam": other}, device_id_type=MESH)

    @pl.when(has_before)
    def _():
        for rim in rims:
            rim.start()

    @pl.when(works)
    def _():
        for copy in loads:
            copy.start()

    @pl.loop(0, slots)
    def _(j):
        x, y = ox_ref[j], oy_ref[j]
        cut_rows[j] = picks((low, low + n), x, 1)
        cut_columns[j] = picks((wide, n), y, 0)
        put_columns[j] = picks((n, wide), y, 1)
        put_rows[j, 0] = picks((n, n), x, 0)
        put_rows[j, 1] = picks((n, n), x - n, 0)

    def block_copy(j):
        return pltpu.make_async_remote_copy(
            src_ref=blocks.at[j],
            dst_ref=trans.at[me],
            send_sem=block_send.at[j],
            recv_sem=block_recv.at[me],
            device_id={"beam": host(j)},
            device_id_type=MESH,
        )

    def half_copy(j, h):
        rows = slice(h * low, (h + 1) * low)
        return pltpu.make_async_remote_copy(
            src_ref=blocks.at[j, :, rows],
            dst_ref=trans.at[me, :, rows],
            send_sem=block_send.at[j],
            recv_sem=block_recv.at[me],
            device_id={"beam": host(j)},
            device_id_type=MESH,
        )

    group = 8
    for h in (0, 1):
        rows = slice(h * low, (h + 1) * low)

        @pl.when(has_after)
        def _(h=h):
            rims[h].wait_recv()

        @pl.when(jnp.logical_not(has_after))
        def _(h=h):
            ext[:, n + h * low : n + (h + 1) * low] = jnp.zeros((2, low, wide), BF16)

        @pl.loop(0, slots // group)
        def _(g, h=h, rows=rows):
            members = [g * group + m for m in range(group)]
            lines = jnp.concatenate([cut_rows[j] for j in members], axis=0)
            picked = [
                dot(lines, ext[part, h * low : h * low + low + n]).astype(BF16) for part in (0, 1)
            ]
            for m, j in enumerate(members):
                own = slice(m * low, (m + 1) * low)
                both = jnp.concatenate([picked[0][own], picked[1][own]], axis=0)
                both = dot(both, cut_columns[j]).astype(BF16)
                blocks[j, 0, rows] = both[:low]
                blocks[j, 1, rows] = both[low:]
            for j in members:

                @pl.when(host(j) < me)
                def _(j=j):
                    half_copy(j, h).start()

                if h == 1:

                    @pl.when(host(j) == me)
                    def _(j=j):
                        pltpu.make_async_copy(blocks.at[j], trans.at[me], block_recv.at[me]).start()

    @pl.loop(me + 1, n_beam)
    def _(other):
        @pl.when(meets(me, other))
        def _():
            pl.semaphore_wait(here.at[other], 1)

            @pl.when(hosts(other))
            def _():
                block_copy(slot_of(other)).start()

    def grad_copy(k):
        return pltpu.make_async_remote_copy(
            src_ref=sent.at[k],
            dst_ref=landed.at[slot],
            send_sem=grad_send.at[k],
            recv_sem=grad_recv.at[slot],
            device_id={"beam": k},
            device_id_type=MESH,
        )

    tall = n // ROW_BLOCKS

    def times_trans(k, field):
        out = []
        for b, (re, im) in enumerate(field):
            rows = slice(b * tall, (b + 1) * tall)
            t_re = 1.0 + trans[k, 0, rows].astype(F32)
            t_im = trans[k, 1, rows].astype(F32)
            out.append((t_re * re - t_im * im, t_re * im + t_im * re))
        return out

    def wait_block(k):
        pltpu.make_async_copy(blocks.at[0], trans.at[k], block_recv.at[k]).wait()

    def keep(k, field):
        for b, (re, im) in enumerate(field):
            rows = slice(b * tall, (b + 1) * tall)
            waves[k, 0, rows] = re
            waves[k, 1, rows] = im

    def kept(k):
        return [
            (waves[k, 0, b * tall : (b + 1) * tall], waves[k, 1, b * tall : (b + 1) * tall])
            for b in range(ROW_BLOCKS)
        ]

    def give(k, field):
        for b, ((w_re, w_im), (d_re, d_im)) in enumerate(zip(kept(k), field)):
            rows = slice(b * tall, (b + 1) * tall)
            sent[k, 0, rows] = (w_re * d_re - w_im * d_im).astype(BF16)
            sent[k, 1, rows] = -(w_re * d_im + w_im * d_re).astype(BF16)

    def post(k):
        @pl.when(k != me)
        def _():
            grad_copy(k).start()

        @pl.when(k == me)
        def _():
            pltpu.make_async_copy(sent.at[k], landed.at[slot], grad_recv.at[slot]).start()

    @pl.when(works)
    def _():
        for copy in loads:
            copy.wait()
        wait_block(0)
        half[...] = by_right(times_trans(0, kept(0)), rights.at[0])

        @pl.loop(1, n_beam)
        def _(k):
            wait_block(k)
            field = by_left(lefts.at[0], half[...])
            keep(k, field)
            table = k // (n_beam - 1)
            half[...] = by_right(times_trans(k, field), rights.at[table])

        last = n_beam - 1
        live = jnp.where(slot < count_ref[0], 1.0, 0.0)
        field = []
        for b, (re, im) in enumerate(by_left(lefts.at[1], half[...])):
            misfit = live * (re * re + im * im - measured[b * tall : (b + 1) * tall])
            field.append((misfit * re, -(misfit * im)))
        half[...] = by_right(field, rights.at[1])

        @pl.loop(0, last)
        def _(i):
            k = last - i
            field = by_left(lefts.at[(k + 1) // n_beam], half[...])
            half[...] = by_right(times_trans(k, field), rights.at[0])
            give(k, field)
            post(k)

        give(0, by_left(lefts.at[0], half[...]))
        post(0)

    @pl.loop(0, slots)
    def _(j):
        pltpu.make_async_copy(sent.at[0], landed.at[j], grad_recv.at[j]).wait()
        both = jnp.concatenate([landed[j, 0], landed[j, 1]], axis=0)
        both = dot(both, put_columns[j]).astype(BF16)
        place = pl.ds(pl.multiple_of(j * n, n), n)
        spread[0, place] = both[0:n]
        spread[1, place] = both[n : 2 * n]

    def gathered(part, beyond):
        rows = jnp.concatenate([put_rows[j, beyond] for j in range(slots)], axis=1)
        return dot(rows, spread[part])

    backs = [
        pltpu.make_async_remote_copy(
            src_ref=rim_out.at[part],
            dst_ref=rim_hbm.at[part, 0],
            send_sem=back_send.at[part],
            recv_sem=back_recv.at[part],
            device_id={"lat": after},
            device_id_type=MESH,
        )
        for part in (0, 1)
    ]
    for part in (0, 1):
        rim_out[part] = gathered(part, 1).astype(BF16)

        @pl.when(has_after)
        def _(part=part):
            backs[part].start()

    for part in (0, 1):
        out[part, 0] = gathered(part, 0)
        pltpu.make_async_copy(out.at[part], own_hbm.at[part], store.at[part]).start()

    for part in (0, 1):
        pltpu.make_async_copy(out.at[part], own_hbm.at[part], store.at[part]).wait()

        @pl.when(has_before)
        def _(part=part):
            backs[part].wait_recv()

        @pl.when(has_before)
        def _(part=part):
            rims[part].wait_send()

        @pl.when(has_after)
        def _(part=part):
            backs[part].wait_send()

    @pl.loop(0, slots)
    def _(j):
        @pl.when(host(j) != me)
        def _():
            block_copy(j).wait_send()

    @pl.when(works)
    def _():
        @pl.loop(0, n_beam)
        def _(k):
            @pl.when(k != me)
            def _():
                grad_copy(k).wait_send()


def on_device(n_beam, n_lat, contrast, probe, offset_x, offset_y, probe_count, measured):
    slots, n = measured.shape[0], measured.shape[1]
    wide = contrast.shape[3]
    rights, lefts = host_tables(n)
    smem = pl.BlockSpec(memory_space=pltpu.SMEM)
    hbm = pl.BlockSpec(memory_space=pltpu.HBM)
    dma = pltpu.SemaphoreType.DMA
    own, rim = pl.pallas_call(
        functools.partial(kernel, n_beam=n_beam, n_lat=n_lat),
        out_shape=[
            jax.ShapeDtypeStruct(contrast.shape, F32),
            jax.ShapeDtypeStruct(contrast.shape, BF16),
        ],
        in_specs=[smem] * 3 + [hbm] * 5,
        out_specs=[hbm, hbm],
        scratch_shapes=[
            pltpu.VMEM(contrast.shape, F32),
            pltpu.VMEM((n, n), F32),
            pltpu.VMEM(rights.shape, BF16),
            pltpu.VMEM(lefts.shape, BF16),
            pltpu.VMEM((2, 2 * n, wide), BF16),
            pltpu.VMEM((slots, n // 2, n // 2 + n), BF16),
            pltpu.VMEM((slots, wide, n), BF16),
            pltpu.VMEM((slots, n, wide), BF16),
            pltpu.VMEM((slots, 2, n, n), BF16),
            pltpu.VMEM((slots, 2, n, n), BF16),
            pltpu.VMEM((n_beam, 2, n, n), BF16),
            pltpu.VMEM((n_beam, 2, n, n), F32),
            pltpu.VMEM((2 * n, 2 * n), BF16),
            pltpu.VMEM((n_beam, 2, n, n), BF16),
            pltpu.VMEM((slots, 2, n, n), BF16),
            pltpu.VMEM((2, slots * n, wide), BF16),
            pltpu.VMEM((2, n, wide), BF16),
            pltpu.VMEM(contrast.shape, F32),
            dma((5,)),
            dma((2,)),
            dma((slots,)),
            dma((n_beam,)),
            dma((n_beam,)),
            dma((slots,)),
            dma((2,)),
            dma((2,)),
            dma((2,)),
            dma((2,)),
            pltpu.SemaphoreType.REGULAR((n_beam,)),
        ],
        compiler_params=pltpu.CompilerParams(
            collective_id=0, has_side_effects=True, vmem_limit_bytes=60 << 20
        ),
    )(offset_x, offset_y, probe_count, contrast, probe, measured, jnp.asarray(rights), jnp.asarray(lefts))
    return own + jnp.where(lax.axis_index("lat") > 0, rim.astype(F32), 0.0)


def solution(mesh):
    in_specs = (
        P(None, "beam", "lat", None),
        P(),
        P("lat"),
        P("lat"),
        P("lat"),
        P("lat", None, None),
    )
    return jax.shard_map(
        functools.partial(on_device, mesh.shape["beam"], mesh.shape["lat"]),
        mesh=mesh,
        in_specs=in_specs,
        out_specs=P(None, "beam", "lat", None),
        check_vma=False,
    )
```
